512 devices in a mesh: row: 32 (over x, y), col: 16 (over z, core).
Axes of the slice: x: 4, y: 8, z: 8, core: 2. Of those that a mesh axis runs over, the one named last changes fastest.
Arguments:
- amplitudes: bfloat16 [32768, 32768], P('row', 'col'), may hold values from -6 to 6
- integrals: bfloat16 [32768, 1024], P('col', 'row'), may hold values from -0.03125 to 0.03125
- tile_mask: int32 [256, 256], P('row', 'col'), may hold values 0 or 1
Outputs:
- residual: bfloat16 [32768, 1024], P('row', 'col')
The draws below stay inside these ranges and needn't reach their ends.
All inputs are finite; a program needn't handle non-finite values. No bound on the sum of `tile_mask` on one device may be relied on, other than what follows from the above.
Results may differ from the reference program's by a relative error of at most 0.001.
Values may be sent and summed in bfloat16 or wider, within the bound.
A program may use at most 64 MiB of HBM per device.

```python
import jax
import jax.numpy as jnp

TILE = 128
AB_COLS = 1024
MT = 256
KT = 256
MROWS = 32768
KDIM = 32768


def place_ends(array, stream_key, smallest, high):
    longest = array.shape.index(max(array.shape))
    spots = []
    for shift in (0, 1):
        where = [jax.random.randint(jax.random.fold_in(stream_key, axis), (), 0, length) for axis, length in enumerate(array.shape)]
        where[longest] = (where[longest] + shift) % array.shape[longest]
        spots.append(tuple(where))
    return array.at[spots[0]].set(smallest).at[spots[1]].set(high)


def shard_levels(key, shape, split, low, largest):
    def one(dim, parts):
        heights = jax.random.uniform(jax.random.fold_in(jax.random.fold_in(key, 6), dim), (parts,), jnp.float32, low / len(split), largest / len(split))
        return jnp.repeat(jnp.exp(heights), shape[dim] // parts).reshape((-1,) + (1,) * (len(shape) - dim - 1))

    gain = one(*split[0])
    for cut in split[1:]:
        gain = gain * one(*cut)
    return gain


def gaussian(rng, dims, deviation, limit, cuts=(), held_as=jnp.bfloat16):
    values = jax.random.normal(rng, dims, jnp.float32) * deviation
    if len(cuts) > 0:
        values = shard_levels(rng, dims, cuts, -0.22, 0.18) * values
    return jnp.clip(values, min=-limit, max=limit).astype(held_as)


def setup_inputs(seed: int = 0) -> dict:
    arg_keys = jax.random.split(jax.random.key(seed), 4)
    amplitudes = gaussian(arg_keys[0], (MROWS, KDIM), 1.0, 6.0, ((0, 32), (1, 16)))
    integrals = gaussian(arg_keys[1], (KDIM, AB_COLS), KDIM ** -0.5, 0.03125, ((0, 16), (1, 32)))
    tile_mask = place_ends((jax.random.randint(arg_keys[2], (MT, KT), 0, 2) < 1).astype(jnp.int32), jax.random.fold_in(arg_keys[2], 1), 0, 1)
    return dict(amplitudes=amplitudes, integrals=integrals, tile_mask=tile_mask)


def reference(amplitudes, integrals, tile_mask):
    tiles_m, tiles_k = tile_mask.shape
    blocks = amplitudes.reshape(tiles_m, TILE, tiles_k, TILE)
    weights = tile_mask.astype(amplitudes.dtype)[:, None, :, None]
    masked = (blocks * weights).reshape(amplitudes.shape)
    return jnp.dot(masked, integrals, preferred_element_type=jnp.float32).astype(jnp.bfloat16)
```

```python
import jax
import jax.numpy as jnp
from jax import lax
from jax.experimental import pallas as pl
from jax.experimental.pallas import tpu as pltpu
from jax.sharding import PartitionSpec as P

MESH = pl.DeviceIdType.MESH
NX, NY, NZ = 4, 8, 8
TILE = 128
SHARD = 32
ROWS = 1024
DEPTH = 2048
HALF = ROWS // 2
BLOCK = 256
SPLIT = 768

FIRST = slice(0, SPLIT)
REST = slice(SPLIT, DEPTH)
FIRST_A = slice(0, SPLIT // 2)
FIRST_B = slice(SPLIT // 2, SPLIT)
REST_A = slice(SPLIT, (SPLIT + DEPTH) // 2)
REST_B = slice((SPLIT + DEPTH) // 2, DEPTH)
N_SEND = 120


def shard(j):
    return slice(j * SHARD, (j + 1) * SHARD)


def kernel(a_hbm, own, mask, out, a, bt, cb, xb, rb, fin, done, lsem, ssem, ag, ex, ch, fs):
    row, col = lax.axis_index("row"), lax.axis_index("col")
    x, y = row // NY, row % NY
    z, core = col // 2, col % 2
    xp = (((x + 1) % NX) * NY + y, col)
    xm = (((x + NX - 1) % NX) * NY + y, col)
    yp = (x * NY + (y + 1) % NY, col)
    ym = (x * NY + (y + NY - 1) % NY, col)
    sigma = 1 - 2 * core
    ahead = (row, ((z + NZ + sigma) % NZ) * 2 + core)
    behind = (row, ((z + NZ - sigma) % NZ) * 2 + core)
    partner = (row, z * 2 + 1 - core)

    load_a = pltpu.make_async_copy(a_hbm, a, lsem.at[0])
    load_b = pltpu.make_async_copy(own, bt.at[0, shard(0)], lsem.at[1])
    load_a.start()
    load_b.start()

    barrier = pltpu.get_barrier_semaphore()
    for dev in (xp, xm, yp, ym, ahead, behind, partner):
        pl.semaphore_signal(barrier, inc=1, device_id=dev, device_id_type=MESH)
    pl.semaphore_wait(barrier, 7)

    pending = []
    count = [0]

    def copy_of(src, dst, send_sem, recv_sem, dev):
        return pltpu.make_async_remote_copy(
            src_ref=src, dst_ref=dst, send_sem=send_sem, recv_sem=recv_sem, device_id=dev, device_id_type=MESH
        )

    def send(src, dst, recv_sem, dev):
        copy = copy_of(src, dst, ssem.at[count[0]], recv_sem, dev)
        count[0] += 1
        copy.start()
        pending.append((None, copy))

    def arrive(dst, recv_sem):
        copy_of(dst, dst, ssem.at[0], recv_sem, partner).wait_recv()

    def origin(q):
        step = (q + 1) // 2
        return (y + NY - step) % NY if q % 2 == 1 else (y + step) % NY

    def own_sends():
        for dev, j, k in ((xp, 3, 2), (xm, 1, 3)):
            send(own.at[:, FIRST], bt.at[0, shard(j), FIRST], ag.at[0, k], dev)
        for dev, q in ((yp, 1), (ym, 2)):
            send(own.at[:, REST], bt.at[q, shard(0), REST], ag.at[q, 0], dev)
            send(own.at[:, FIRST], bt.at[q, shard(0), FIRST], ag.at[q, 2], dev)
        for dev, j, k in ((xp, 3, 6), (xm, 1, 7)):
            send(own.at[:, REST], bt.at[0, shard(j), REST], ag.at[0, k], dev)

    def own_gather():
        arrive(bt.at[0, shard(3), FIRST], ag.at[0, 2])
        send(bt.at[0, shard(3), FIRST_A], bt.at[0, shard(2), FIRST_A], ag.at[0, 4], xp)
        for dev, q in ((yp, 1), (ym, 2)):
            send(bt.at[0, shard(3), FIRST], bt.at[q, shard(3), FIRST], ag.at[q, 5], dev)
        arrive(bt.at[0, shard(1), FIRST], ag.at[0, 3])
        send(bt.at[0, shard(1), FIRST_B], bt.at[0, shard(2), FIRST_B], ag.at[0, 5], xm)
        for dev, q in ((yp, 1), (ym, 2)):
            send(bt.at[0, shard(1), FIRST], bt.at[q, shard(1), FIRST], ag.at[q, 3], dev)

    def own_gather_far():
        arrive(bt.at[0, shard(2), FIRST_A], ag.at[0, 4])
        arrive(bt.at[0, shard(2), FIRST_B], ag.at[0, 5])
        for dev, q in ((yp, 1), (ym, 2)):
            send(bt.at[0, shard(2), FIRST], bt.at[q, shard(2), FIRST], ag.at[q, 4], dev)

    def across(q):
        send(bt.at[q, shard(0), REST], bt.at[q, shard(3), REST], ag.at[q, 6], xp)
        send(bt.at[q, shard(0), REST], bt.at[q, shard(1), REST], ag.at[q, 7], xm)

    def take_rest(q):
        if q == 7:
            arrive(bt.at[7, shard(0), REST_A], ag.at[7, 0])
            arrive(bt.at[7, shard(0), REST_B], ag.at[7, 1])
            across(7)
            return
        dev = yp if q % 2 == 1 else ym
        arrive(bt.at[q, shard(0), REST], ag.at[q, 0])
        if q < 5:
            send(bt.at[q, shard(0), REST], bt.at[q + 2, shard(0), REST], ag.at[q + 2, 0], dev)
        elif q == 5:
            send(bt.at[5, shard(0), REST_A], bt.at[7, shard(0), REST_A], ag.at[7, 0], dev)
        else:
            send(bt.at[6, shard(0), REST_B], bt.at[7, shard(0), REST_B], ag.at[7, 1], dev)
        across(q)

    def take_first(q, j):
        dev = yp if q % 2 == 1 else ym
        arrive(bt.at[q, shard(j), FIRST], ag.at[q, 2 + j])
        if q < 5:
            send(bt.at[q, shard(j), FIRST], bt.at[q + 2, shard(j), FIRST], ag.at[q + 2, 2 + j], dev)
        elif (q == 5 and j in (0, 3)) or (q == 6 and j in (1, 2)):
            send(bt.at[q, shard(j), FIRST], bt.at[7, shard(j), FIRST], ag.at[7, 2 + j], dev)

    def relay(q):
        arrive(bt.at[q, shard(3), REST], ag.at[q, 6])
        send(bt.at[q, shard(3), REST_A], bt.at[q, shard(2), REST_A], ag.at[q, 8], xp)
        arrive(bt.at[q, shard(1), REST], ag.at[q, 7])
        send(bt.at[q, shard(1), REST_B], bt.at[q, shard(2), REST_B], ag.at[q, 9], xm)

    def take_far(q):
        arrive(bt.at[q, shard(2), REST_A], ag.at[q, 8])
        arrive(bt.at[q, shard(2), REST_B], ag.at[q, 9])

    def multiply(q, which, i):
        start = pl.multiple_of(which * HALF + i * BLOCK, BLOCK)
        cb[q, which, :, i * BLOCK : (i + 1) * BLOCK] = lax.dot_general(
            bt[q], a[pl.ds(start, BLOCK), :], (((1,), (1,)), ((), ())), preferred_element_type=jnp.float32
        )

    def swap(q):
        send(cb.at[q, 1 - core], xb.at[q], ex.at[q], partner)

    def spot(q, delta):
        h = origin(q) // 4
        e = (z + NZ - h) % NZ
        j = ((e + delta + NZ) // 2 + NX - x) % NX
        return cb.at[q, core, pl.ds(pl.multiple_of(j * SHARD, SHARD), SHARD), :]

    def is_even(q):
        return (z + origin(q) // 4) % 2 == 0

    base = 84

    def pass_on(q, cond, src, slot, sem, dev):
        copy = copy_of(src, rb.at[q, slot], ssem.at[base + 4 * q + sem], ch.at[q, slot], dev)
        copy.start()
        pending.append((cond, copy))

    def merge(q):
        arrive(xb.at[q], ex.at[q])
        cb[q, core] += xb[q]

    def stage1(q):
        even = is_even(q)

        @pl.when(even)
        def _():
            pass_on(q, "even", spot(q, 4), 0, 0, ahead)

    def stage2(q):
        even = is_even(q)

        @pl.when(jnp.logical_not(even))
        def _():
            pass_on(q, "odd", spot(q, -3 * sigma), 1, 1, behind)
            arrive(rb.at[q, 0], ch.at[q, 0])
            here = spot(q, 3 * sigma)
            here[...] += rb[q, 0]
            pass_on(q, "odd", here, 0, 0, ahead)

    def stage3(q):
        even = is_even(q)

        @pl.when(even)
        def _():
            for slot, sign, dev in ((1, -1, behind), (0, 1, ahead)):
                arrive(rb.at[q, slot], ch.at[q, slot])
                here = spot(q, 2 * sign * sigma)
                here[...] += rb[q, slot]
                pass_on(q, "even", here, 2 + slot, 1 + slot, dev)

    def stage4(q):
        even = is_even(q)

        @pl.when(jnp.logical_not(even))
        def _():
            for slot, sign, dev in ((1, -1, behind), (0, 1, ahead)):
                arrive(rb.at[q, 2 + slot], ch.at[q, 2 + slot])
                here = spot(q, sign * sigma)
                here[...] += rb[q, 2 + slot]
                pass_on(q, "odd", here, 2 + slot, 2 + slot, dev)

    def place(ref, index):
        columns = pl.ds(pl.multiple_of(core * HALF, HALF), HALF)
        return ref.at[index, :, columns]

    def finish(q):
        even = is_even(q)
        origin_y = origin(q)
        index = origin_y % 2
        mine = (origin_y // 2) % 2 == core

        @pl.when(even)
        def _():
            arrive(rb.at[q, 2], ch.at[q, 2])
            arrive(rb.at[q, 3], ch.at[q, 3])
            total = (spot(q, 0)[...] + rb[q, 2] + rb[q, 3]).astype(jnp.bfloat16)

            @pl.when(mine)
            def _():
                place(done, index)[...] = total

            @pl.when(jnp.logical_not(mine))
            def _():
                fin[index] = total
                copy_of(fin.at[index], place(done, index), fs.at[0, index], fs.at[1, index], partner).start()

    own_sends()
    own_gather()
    load_a.wait()

    def apply_mask(i, carry):
        rows = pl.ds(pl.multiple_of(i * TILE, TILE), TILE)
        for k in range(DEPTH // TILE):
            cols = slice(k * TILE, (k + 1) * TILE)
            a[rows, cols] = jnp.where(mask[i, k] != 0, a[rows, cols], jnp.zeros((TILE, TILE), jnp.bfloat16))
        return carry

    lax.fori_loop(0, ROWS // TILE, apply_mask, 0)
    own_gather_far()
    load_b.wait()

    for t in range(1, 15):
        for q, step in ((t - 7, finish), (t - 6, stage4), (t - 5, stage3), (t - 4, stage2)):
            if 0 <= q < 8:
                step(q)
        if 0 <= t - 3 < 8:
            merge(t - 3)
            stage1(t - 3)
        if 0 <= t - 1 < 8:
            relay(t - 1)
        work = []
        if 0 <= t - 2 < 8:
            q = t - 2
            take_far(q)
            work = [(q, 1 - core, 0), (q, 1 - core, 1), (q, core, 0), (q, core, 1)]
        takes = []
        if t < 8:
            takes = [None] + [0, 3, 1, 2]
        for i in range(5):
            if i < len(takes):
                if takes[i] is None:
                    take_rest(t)
                else:
                    take_first(t, takes[i])
            if i < len(work):
                multiply(*work[i])
                if i == 1:
                    swap(t - 2)

    for index in range(2):
        @pl.when(True)
        def _():
            half = pl.ds(pl.multiple_of((1 - core) * HALF, HALF), HALF)
            arrive(done.at[index, :, half], fs.at[1, index])
            copy_of(fin.at[index], place(done, index), fs.at[0, index], fs.at[1, index], partner).wait_send()
    for index in range(2):
        out[index * SHARD : (index + 1) * SHARD, :] = done[index]

    for cond, copy in pending:
        if cond is None:
            copy.wait_send()
    for q in range(8):
        even = is_even(q)
        parts = {"even": [c for p, c in pending if p == "even"], "odd": [c for p, c in pending if p == "odd"]}
        del parts

        @pl.when(even)
        def _():
            for slot in range(3):
                copy_of(rb.at[q, 0], rb.at[q, 0], ssem.at[base + 4 * q + slot], ch.at[q, 0], partner).wait_send()

        @pl.when(jnp.logical_not(even))
        def _():
            for slot in range(4):
                copy_of(rb.at[q, 0], rb.at[q, 0], ssem.at[base + 4 * q + slot], ch.at[q, 0], partner).wait_send()


def per_device(amplitudes, integrals, tile_mask):
    result = pl.pallas_call(
        kernel,
        out_shape=jax.ShapeDtypeStruct((2 * SHARD, ROWS), jnp.bfloat16),
        in_specs=[
            pl.BlockSpec(memory_space=pl.ANY),
            pl.BlockSpec(memory_space=pl.ANY),
            pl.BlockSpec(memory_space=pltpu.SMEM),
        ],
        out_specs=pl.BlockSpec(memory_space=pltpu.VMEM),
        scratch_shapes=[
            pltpu.VMEM((ROWS, DEPTH), jnp.bfloat16),
            pltpu.VMEM((8, 4 * SHARD, DEPTH), jnp.bfloat16),
            pltpu.VMEM((8, 2, 4 * SHARD, HALF), jnp.float32),
            pltpu.VMEM((8, 4 * SHARD, HALF), jnp.float32),
            pltpu.VMEM((8, 4, SHARD, HALF), jnp.float32),
            pltpu.VMEM((2, SHARD, HALF), jnp.bfloat16),
            pltpu.VMEM((2, SHARD, ROWS), jnp.bfloat16),
            pltpu.SemaphoreType.DMA((2,)),
            pltpu.SemaphoreType.DMA((N_SEND,)),
            pltpu.SemaphoreType.DMA((8, 10)),
            pltpu.SemaphoreType.DMA((8,)),
            pltpu.SemaphoreType.DMA((8, 4)),
            pltpu.SemaphoreType.DMA((2, 2)),
        ],
        compiler_params=pltpu.CompilerParams(
            collective_id=0, has_side_effects=True, vmem_limit_bytes=60 * 1024 * 1024
        ),
    )(amplitudes, integrals.T, tile_mask)
    return result.T


def solution(mesh):
    placed = (P("row", "col"), P("col", "row"), P("row", "col"))
    return jax.shard_map(
        per_device, mesh=mesh, in_specs=placed, out_specs=P("row", "col"), check_vma=False
    )
```

```python
import jax
import jax.numpy as jnp
from jax import lax
from jax.experimental import pallas as pl
from jax.experimental.pallas import tpu as pltpu
from jax.sharding import PartitionSpec as P

MESH = pl.DeviceIdType.MESH
NX, NY, NZ = 4, 8, 8
TILE = 128
SHARD = 32
ROWS = 1024
DEPTH = 2048
HALF = ROWS // 2
BLOCK = 256
SPLIT = 768

FIRST = slice(0, SPLIT)
REST = slice(SPLIT, DEPTH)
FIRST_A = slice(0, SPLIT // 2)
FIRST_B = slice(SPLIT // 2, SPLIT)
REST_A = slice(SPLIT, (SPLIT + DEPTH) // 2)
REST_B = slice((SPLIT + DEPTH) // 2, DEPTH)
BASE = 100
N_SEND = BASE + 32
FAST = (7,)


def shard(j):
    return slice(j * SHARD, (j + 1) * SHARD)


def kernel(a_hbm, own, mask, out, a, bt, cb, xb, rb, fb, fin, done, lsem, ssem, ag, ex, ch, fch, fs):
    row, col = lax.axis_index("row"), lax.axis_index("col")
    x, y = row // NY, row % NY
    z, core = col // 2, col % 2
    xp = (((x + 1) % NX) * NY + y, col)
    xm = (((x + NX - 1) % NX) * NY + y, col)
    yp = (x * NY + (y + 1) % NY, col)
    ym = (x * NY + (y + NY - 1) % NY, col)
    sigma = 1 - 2 * core
    ahead = (row, ((z + NZ + sigma) % NZ) * 2 + core)
    behind = (row, ((z + NZ - sigma) % NZ) * 2 + core)
    partner = (row, z * 2 + 1 - core)

    def along_z(delta):
        return (row, ((z + NZ + delta) % NZ) * 2 + core)


    load_a = pltpu.make_async_copy(a_hbm, a, lsem.at[0])
    load_b = pltpu.make_async_copy(own, bt.at[0, shard(0)], lsem.at[1])
    load_a.start()
    load_b.start()

    barrier = pltpu.get_barrier_semaphore()
    for dev in [xp, xm, yp, ym, partner] + [along_z(d) for d in (1, -1, 2, -2, 3, -3)]:
        pl.semaphore_signal(barrier, inc=1, device_id=dev, device_id_type=MESH)
    pl.semaphore_wait(barrier, 11)

    pending = []
    count = [0]

    def copy_of(src, dst, send_sem, recv_sem, dev):
        return pltpu.make_async_remote_copy(
            src_ref=src, dst_ref=dst, send_sem=send_sem, recv_sem=recv_sem, device_id=dev, device_id_type=MESH
        )

    def send(src, dst, recv_sem, dev):
        copy = copy_of(src, dst, ssem.at[count[0]], recv_sem, dev)
        count[0] += 1
        copy.start()
        pending.append(copy)

    def arrive(dst, recv_sem):
        copy_of(dst, dst, ssem.at[0], recv_sem, partner).wait_recv()

    def origin(q):
        step = (q + 1) // 2
        return (y + NY - step) % NY if q % 2 == 1 else (y + step) % NY

    def own_first_x():
        for dev, j, k in ((xp, 3, 2), (xm, 1, 3)):
            send(own.at[:, FIRST], bt.at[0, shard(j), FIRST], ag.at[0, k], dev)

    def own_rest_y():
        for dev, q in ((yp, 1), (ym, 2)):
            send(own.at[:, REST], bt.at[q, shard(0), REST], ag.at[q, 0], dev)

    def own_first_y():
        for dev, q in ((yp, 1), (ym, 2)):
            send(own.at[:, FIRST], bt.at[q, shard(0), FIRST], ag.at[q, 2], dev)

    def across_a(q, src):
        send(src.at[:, REST_A], bt.at[q, shard(3), REST_A], ag.at[q, 6], xp)
        send(src.at[:, REST_A], bt.at[q, shard(1), REST_A], ag.at[q, 10], xm)

    def across_b(q, src):
        send(src.at[:, REST_B], bt.at[q, shard(1), REST_B], ag.at[q, 7], xm)
        send(src.at[:, REST_B], bt.at[q, shard(3), REST_B], ag.at[q, 11], xp)

    def across(q, src):
        send(src.at[:, REST_A], bt.at[q, shard(3), REST_A], ag.at[q, 6], xp)
        send(src.at[:, REST_B], bt.at[q, shard(1), REST_B], ag.at[q, 7], xm)
        send(src.at[:, REST_B], bt.at[q, shard(3), REST_B], ag.at[q, 11], xp)
        send(src.at[:, REST_A], bt.at[q, shard(1), REST_A], ag.at[q, 10], xm)

    def own_rest_x():
        across(0, own)

    def gather(j):
        dev, half, k = (xp, FIRST_A, 4) if j == 3 else (xm, FIRST_B, 5)
        arrive(bt.at[0, shard(j), FIRST], ag.at[0, 2 if j == 3 else 3])
        send(bt.at[0, shard(j), half], bt.at[0, shard(2), half], ag.at[0, k], dev)
        for dev, q in ((yp, 1), (ym, 2)):
            send(bt.at[0, shard(j), FIRST], bt.at[q, shard(j), FIRST], ag.at[q, 2 + j], dev)

    def gather_far():
        arrive(bt.at[0, shard(2), FIRST_A], ag.at[0, 4])
        arrive(bt.at[0, shard(2), FIRST_B], ag.at[0, 5])
        for dev, q in ((yp, 1), (ym, 2)):
            send(bt.at[0, shard(2), FIRST], bt.at[q, shard(2), FIRST], ag.at[q, 4], dev)

    def take_rest(q):
        dev = yp if q % 2 == 1 else ym
        arrive(bt.at[q, shard(0), REST], ag.at[q, 0])
        if q < 5:
            send(bt.at[q, shard(0), REST], bt.at[q + 2, shard(0), REST], ag.at[q + 2, 0], dev)
        elif q == 5:
            send(bt.at[5, shard(0), REST_A], bt.at[7, shard(0), REST_A], ag.at[7, 0], dev)
        else:
            send(bt.at[6, shard(0), REST_B], bt.at[7, shard(0), REST_B], ag.at[7, 1], dev)
        across(q, bt.at[q, shard(0)])

    def take_rest_far(source):
        if source == 5:
            arrive(bt.at[7, shard(0), REST_A], ag.at[7, 0])
            across_a(7, bt.at[7, shard(0)])
        else:
            arrive(bt.at[7, shard(0), REST_B], ag.at[7, 1])
            across_b(7, bt.at[7, shard(0)])

    def take_first(q, j):
        dev = yp if q % 2 == 1 else ym
        arrive(bt.at[q, shard(j), FIRST], ag.at[q, 2 + j])
        if q < 5:
            send(bt.at[q, shard(j), FIRST], bt.at[q + 2, shard(j), FIRST], ag.at[q + 2, 2 + j], dev)
        elif (q == 5 and j in (0, 3)) or (q == 6 and j in (1, 2)):
            send(bt.at[q, shard(j), FIRST], bt.at[7, shard(j), FIRST], ag.at[7, 2 + j], dev)

    def relay(q, j):
        if j == 3:
            arrive(bt.at[q, shard(3), REST_A], ag.at[q, 6])
            send(bt.at[q, shard(3), REST_A], bt.at[q, shard(2), REST_A], ag.at[q, 8], xp)
        else:
            arrive(bt.at[q, shard(1), REST_B], ag.at[q, 7])
            send(bt.at[q, shard(1), REST_B], bt.at[q, shard(2), REST_B], ag.at[q, 9], xm)

    def take_far(q):
        arrive(bt.at[q, shard(1), REST_A], ag.at[q, 10])
        arrive(bt.at[q, shard(3), REST_B], ag.at[q, 11])
        arrive(bt.at[q, shard(2), REST_A], ag.at[q, 8])
        arrive(bt.at[q, shard(2), REST_B], ag.at[q, 9])

    def product(q, i):
        if q == 0 and i == 0:
            load_b.wait()
        multiply(q, 1 - core if i < 2 else core, i % 2)
        if i == 1:
            swap(q)

    def multiply(q, which, i):
        start = pl.multiple_of(which * HALF + i * BLOCK, BLOCK)
        cb[q, which, :, i * BLOCK : (i + 1) * BLOCK] = lax.dot_general(
            bt[q], a[pl.ds(start, BLOCK), :], (((1,), (1,)), ((), ())), preferred_element_type=jnp.float32
        )

    def swap(q):
        send(cb.at[q, 1 - core], xb.at[q], ex.at[q], partner)

    def spot(q, delta):
        h = origin(q) // 4
        e = (z + NZ - h) % NZ
        j = ((e + delta + NZ) // 2 + NX - x) % NX
        return cb.at[q, core, pl.ds(pl.multiple_of(j * SHARD, SHARD), SHARD), :]

    def is_even(q):
        return (z + origin(q) // 4) % 2 == 0

    base = BASE

    def pass_on(q, src, slot, sem, dev):
        copy_of(src, rb.at[q, slot], ssem.at[base + 4 * q + sem], ch.at[q, slot], dev).start()

    def merge(q):
        arrive(xb.at[q], ex.at[q])
        cb[q, core] += xb[q]

    def stage1(q):
        even = is_even(q)

        @pl.when(even)
        def _():
            pass_on(q, spot(q, 4), 0, 0, ahead)

    def stage2(q):
        even = is_even(q)

        @pl.when(jnp.logical_not(even))
        def _():
            pass_on(q, spot(q, -3 * sigma), 1, 1, behind)
            arrive(rb.at[q, 0], ch.at[q, 0])
            here = spot(q, 3 * sigma)
            here[...] += rb[q, 0]
            pass_on(q, here, 0, 0, ahead)

    def stage3(q):
        even = is_even(q)

        @pl.when(even)
        def _():
            for slot, sign, dev in ((1, -1, behind), (0, 1, ahead)):
                arrive(rb.at[q, slot], ch.at[q, slot])
                here = spot(q, 2 * sign * sigma)
                here[...] += rb[q, slot]
                pass_on(q, here, 2 + slot, 1 + slot, dev)

    def stage4(q):
        even = is_even(q)

        @pl.when(jnp.logical_not(even))
        def _():
            for slot, sign, dev in ((1, -1, behind), (0, 1, ahead)):
                arrive(rb.at[q, 2 + slot], ch.at[q, 2 + slot])
                here = spot(q, sign * sigma)
                here[...] += rb[q, 2 + slot]
                pass_on(q, here, 2 + slot, 2 + slot, dev)

    def straight(q, src, slot, sem, dev):
        f = FAST.index(q)
        copy_of(src, fb.at[f, slot], ssem.at[base + 4 * q + sem], fch.at[f, slot], dev).start()

    def fast1(q):
        even = is_even(q)

        @pl.when(even)
        def _():
            straight(q, spot(q, 4), 0, 0, ahead)
            straight(q, spot(q, 2), 3, 1, along_z(2))
            straight(q, spot(q, -2), 4, 2, along_z(-2))

        @pl.when(jnp.logical_not(even))
        def _():
            straight(q, spot(q, -3 * sigma), 5 + (1 + sigma) // 2, 0, along_z(-3 * sigma))
            straight(q, spot(q, 1), 1, 1, along_z(1))
            straight(q, spot(q, -1), 2, 2, along_z(-1))

    def fast2(q):
        even = is_even(q)

        @pl.when(jnp.logical_not(even))
        def _():
            f = FAST.index(q)
            arrive(fb.at[f, 0], fch.at[f, 0])
            here = spot(q, 3 * sigma)
            here[...] += fb[f, 0]
            straight(q, here, 5 + (1 - sigma) // 2, 3, along_z(3 * sigma))

    def place(ref, index):
        columns = pl.ds(pl.multiple_of(core * HALF, HALF), HALF)
        return ref.at[index, :, columns]

    def finish(q):
        even = is_even(q)
        origin_y = origin(q)
        index = origin_y % 2
        mine = (origin_y // 2) % 2 == core

        @pl.when(even)
        def _():
            total = spot(q, 0)[...]
            if q in FAST:
                f = FAST.index(q)
                for slot in range(1, 7):
                    arrive(fb.at[f, slot], fch.at[f, slot])
                    total += fb[f, slot]
            else:
                for slot in (2, 3):
                    arrive(rb.at[q, slot], ch.at[q, slot])
                    total += rb[q, slot]
            total = total.astype(jnp.bfloat16)

            @pl.when(mine)
            def _():
                place(done, index)[...] = total

            @pl.when(jnp.logical_not(mine))
            def _():
                fin[index] = total
                copy_of(fin.at[index], place(done, index), fs.at[0, index], fs.at[1, index], partner).start()

    def mask_rows(part):
        if part == 0:
            load_a.wait()

        def apply_mask(i, carry):
            rows = pl.ds(pl.multiple_of(i * TILE, TILE), TILE)
            for k in range(DEPTH // TILE):
                cols = slice(k * TILE, (k + 1) * TILE)
                a[rows, cols] = jnp.where(mask[i, k] != 0, a[rows, cols], jnp.zeros((TILE, TILE), jnp.bfloat16))
            return carry

        lax.fori_loop(4 * part, 4 * part + 4, apply_mask, 0)

    for step, *args in (
        (own_rest_y,),
        (own_first_x,),
        (own_first_y,),
        (own_rest_x,),
        (mask_rows, 0),
        (gather, 1),
        (gather, 3),
        (take_rest, 2),
        (take_rest, 1),
        (take_first, 1, 0),
        (relay, 0, 3),
        (relay, 0, 1),
        (take_first, 2, 0),
        (gather_far,),
        (mask_rows, 1),
        (relay, 2, 1),
        (take_first, 2, 1),
        (relay, 2, 3),
        (relay, 1, 3),
        (relay, 1, 1),
        (take_first, 1, 3),
        (take_rest, 4),
        (take_first, 2, 3),
        (take_rest, 3),
        (take_first, 1, 1),
        (take_far, 0),
        (product, 0, 0),
        (product, 0, 1),
        (take_far, 2),
        (take_first, 2, 2),
        (product, 2, 0),
        (take_first, 1, 2),
        (take_first, 4, 0),
        (product, 0, 2),
        (product, 2, 1),
        (product, 0, 3),
        (take_first, 3, 0),
        (take_far, 1),
        (relay, 4, 3),
        (relay, 4, 1),
        (merge, 0),
        (product, 2, 2),
        (take_first, 4, 1),
        (take_rest, 6),
        (stage1, 0),
        (product, 2, 3),
        (product, 1, 0),
        (relay, 3, 1),
        (product, 1, 1),
        (relay, 3, 3),
        (product, 1, 2),
        (take_first, 4, 2),
        (merge, 2),
        (take_first, 4, 3),
        (take_rest, 5),
        (stage1, 2),
        (take_first, 3, 2),
        (take_first, 3, 3),
        (product, 1, 3),
        (take_far, 4),
        (product, 4, 0),
        (take_first, 3, 1),
        (merge, 1),
        (stage1, 1),
        (product, 4, 1),
        (relay, 6, 3),
        (take_first, 5, 0),
        (relay, 6, 1),
        (stage2, 0),
        (product, 4, 2),
        (take_rest_far, 6),
        (take_first, 6, 1),
        (product, 4, 3),
        (take_far, 3),
        (product, 3, 0),
        (product, 3, 1),
        (relay, 5, 1),
        (relay, 5, 3),
        (take_first, 6, 2),
        (product, 3, 2),
        (stage2, 2),
        (take_rest_far, 5),
        (product, 3, 3),
        (merge, 4),
        (merge, 3),
        (take_first, 5, 2),
        (take_first, 6, 3),
        (stage1, 4),
        (stage1, 3),
        (take_first, 6, 0),
        (stage2, 1),
        (take_far, 6),
        (product, 6, 0),
        (product, 6, 1),
        (take_first, 5, 3),
        (product, 6, 2),
        (stage3, 0),
        (product, 6, 3),
        (relay, 7, 1),
        (take_far, 5),
        (take_first, 5, 1),
        (product, 5, 0),
        (product, 5, 1),
        (relay, 7, 3),
        (merge, 6),
        (stage1, 6),
        (stage3, 2),
        (product, 5, 2),
        (product, 5, 3),
        (take_first, 7, 0),
        (merge, 5),
        (stage1, 5),
        (stage2, 3),
        (stage2, 4),
        (stage3, 1),
        (take_first, 7, 1),
        (stage2, 6),
        (take_first, 7, 2),
        (stage4, 0),
        (take_far, 7),
        (take_first, 7, 3),
        (product, 7, 0),
        (product, 7, 1),
        (stage2, 5),
        (product, 7, 2),
        (product, 7, 3),
        (merge, 7),
        (fast1, 7),
        (stage3, 4),
        (stage3, 3),
        (stage3, 5),
        (stage3, 6),
        (stage4, 2),
        (stage4, 1),
        (fast2, 7),
        (stage4, 4),
        (finish, 0),
        (stage4, 3),
        (stage4, 5),
        (stage4, 6),
        (finish, 7),
        (finish, 1),
        (finish, 2),
        (finish, 4),
        (finish, 3),
        (finish, 5),
        (finish, 6),
    ):
        step(*args)

    for index in range(2):
        half = pl.ds(pl.multiple_of((1 - core) * HALF, HALF), HALF)
        arrive(done.at[index, :, half], fs.at[1, index])
        copy_of(fin.at[index], place(done, index), fs.at[0, index], fs.at[1, index], partner).wait_send()
    for index in range(2):
        out[index * SHARD : (index + 1) * SHARD, :] = done[index]

    for copy in pending:
        copy.wait_send()
    for q in range(8):
        even = is_even(q)

        @pl.when(even)
        def _():
            for slot in range(3):
                copy_of(rb.at[q, 0], rb.at[q, 0], ssem.at[base + 4 * q + slot], ch.at[q, 0], partner).wait_send()

        @pl.when(jnp.logical_not(even))
        def _():
            for slot in range(4):
                copy_of(rb.at[q, 0], rb.at[q, 0], ssem.at[base + 4 * q + slot], ch.at[q, 0], partner).wait_send()


def per_device(amplitudes, integrals, tile_mask):
    result = pl.pallas_call(
        kernel,
        out_shape=jax.ShapeDtypeStruct((2 * SHARD, ROWS), jnp.bfloat16),
        in_specs=[
            pl.BlockSpec(memory_space=pl.ANY),
            pl.BlockSpec(memory_space=pl.ANY),
            pl.BlockSpec(memory_space=pltpu.SMEM),
        ],
        out_specs=pl.BlockSpec(memory_space=pltpu.VMEM),
        scratch_shapes=[
            pltpu.VMEM((ROWS, DEPTH), jnp.bfloat16),
            pltpu.VMEM((8, 4 * SHARD, DEPTH), jnp.bfloat16),
            pltpu.VMEM((8, 2, 4 * SHARD, HALF), jnp.float32),
            pltpu.VMEM((8, 4 * SHARD, HALF), jnp.float32),
            pltpu.VMEM((8, 4, SHARD, HALF), jnp.float32),
            pltpu.VMEM((len(FAST), 7, SHARD, HALF), jnp.float32),
            pltpu.VMEM((2, SHARD, HALF), jnp.bfloat16),
            pltpu.VMEM((2, SHARD, ROWS), jnp.bfloat16),
            pltpu.SemaphoreType.DMA((2,)),
            pltpu.SemaphoreType.DMA((N_SEND,)),
            pltpu.SemaphoreType.DMA((8, 12)),
            pltpu.SemaphoreType.DMA((8,)),
            pltpu.SemaphoreType.DMA((8, 4)),
            pltpu.SemaphoreType.DMA((len(FAST), 7)),
            pltpu.SemaphoreType.DMA((2, 2)),
        ],
        compiler_params=pltpu.CompilerParams(
            collective_id=0, has_side_effects=True, vmem_limit_bytes=60 * 1024 * 1024
        ),
    )(amplitudes, integrals.T, tile_mask)
    return result.T


def solution(mesh):
    placed = (P("row", "col"), P("col", "row"), P("row", "col"))
    return jax.shard_map(
        per_device, mesh=mesh, in_specs=placed, out_specs=P("row", "col"), check_vma=False
    )
```

```python
import jax
import jax.numpy as jnp
from jax import lax
from jax.experimental import pallas as pl
from jax.experimental.pallas import tpu as pltpu
from jax.sharding import PartitionSpec as P

MESH = pl.DeviceIdType.MESH
NX, NY, NZ = 4, 8, 8
TILE = 128
SHARD = 32
ROWS = 1024
DEPTH = 2048
HALF = ROWS // 2
LEVELS = 32000.0
CODED = SHARD * HALF // TILE + 16
BLOCK = 256
SPLIT = 768

FIRST = slice(0, SPLIT)
REST = slice(SPLIT, DEPTH)
FIRST_A = slice(0, SPLIT // 2)
FIRST_B = slice(SPLIT // 2, SPLIT)
REST_A = slice(SPLIT, (SPLIT + DEPTH) // 2)
REST_B = slice((SPLIT + DEPTH) // 2, DEPTH)
BASE = 100
N_SEND = BASE + 32
FAST = (6, 7)


def shard(j):
    return slice(j * SHARD, (j + 1) * SHARD)


def kernel(a_hbm, own, mask, out, a, bt, cb, xb, eb, rb, fb, fin, done, lsem, ssem, ag, ex, ch, fch, fs):
    row, col = lax.axis_index("row"), lax.axis_index("col")
    x, y = row // NY, row % NY
    z, core = col // 2, col % 2
    xp = (((x + 1) % NX) * NY + y, col)
    xm = (((x + NX - 1) % NX) * NY + y, col)
    yp = (x * NY + (y + 1) % NY, col)
    ym = (x * NY + (y + NY - 1) % NY, col)
    sigma = 1 - 2 * core
    ahead = (row, ((z + NZ + sigma) % NZ) * 2 + core)
    behind = (row, ((z + NZ - sigma) % NZ) * 2 + core)
    partner = (row, z * 2 + 1 - core)

    def along_z(delta):
        return (row, ((z + NZ + delta) % NZ) * 2 + core)


    load_a = pltpu.make_async_copy(a_hbm, a, lsem.at[0])
    load_b = pltpu.make_async_copy(own, bt.at[0, shard(0)], lsem.at[1])
    load_a.start()
    load_b.start()

    barrier = pltpu.get_barrier_semaphore()
    for dev in [xp, xm, yp, ym, partner] + [along_z(d) for d in (1, -1, 2, -2, 3, -3)]:
        pl.semaphore_signal(barrier, inc=1, device_id=dev, device_id_type=MESH)
    pl.semaphore_wait(barrier, 11)

    pending = []
    count = [0]

    def copy_of(src, dst, send_sem, recv_sem, dev):
        return pltpu.make_async_remote_copy(
            src_ref=src, dst_ref=dst, send_sem=send_sem, recv_sem=recv_sem, device_id=dev, device_id_type=MESH
        )

    def send(src, dst, recv_sem, dev):
        copy = copy_of(src, dst, ssem.at[count[0]], recv_sem, dev)
        count[0] += 1
        copy.start()
        pending.append(copy)

    def arrive(dst, recv_sem):
        copy_of(dst, dst, ssem.at[0], recv_sem, partner).wait_recv()

    def origin(q):
        step = (q + 1) // 2
        return (y + NY - step) % NY if q % 2 == 1 else (y + step) % NY

    def own_first_x():
        for dev, j, k in ((xp, 3, 2), (xm, 1, 3)):
            send(own.at[:, FIRST], bt.at[0, shard(j), FIRST], ag.at[0, k], dev)

    def own_rest_y():
        for dev, q in ((yp, 1), (ym, 2)):
            send(own.at[:, REST], bt.at[q, shard(0), REST], ag.at[q, 0], dev)

    def own_first_y():
        for dev, q in ((yp, 1), (ym, 2)):
            send(own.at[:, FIRST], bt.at[q, shard(0), FIRST], ag.at[q, 2], dev)

    def across_a(q, src):
        send(src.at[:, REST_A], bt.at[q, shard(3), REST_A], ag.at[q, 6], xp)
        send(src.at[:, REST_A], bt.at[q, shard(1), REST_A], ag.at[q, 10], xm)

    def across_b(q, src):
        send(src.at[:, REST_B], bt.at[q, shard(1), REST_B], ag.at[q, 7], xm)
        send(src.at[:, REST_B], bt.at[q, shard(3), REST_B], ag.at[q, 11], xp)

    def across(q, src):
        send(src.at[:, REST_A], bt.at[q, shard(3), REST_A], ag.at[q, 6], xp)
        send(src.at[:, REST_B], bt.at[q, shard(1), REST_B], ag.at[q, 7], xm)
        send(src.at[:, REST_B], bt.at[q, shard(3), REST_B], ag.at[q, 11], xp)
        send(src.at[:, REST_A], bt.at[q, shard(1), REST_A], ag.at[q, 10], xm)

    def own_rest_x():
        across(0, own)

    def gather(j):
        dev, half, k = (xp, FIRST_A, 4) if j == 3 else (xm, FIRST_B, 5)
        arrive(bt.at[0, shard(j), FIRST], ag.at[0, 2 if j == 3 else 3])
        send(bt.at[0, shard(j), half], bt.at[0, shard(2), half], ag.at[0, k], dev)
        for dev, q in ((yp, 1), (ym, 2)):
            send(bt.at[0, shard(j), FIRST], bt.at[q, shard(j), FIRST], ag.at[q, 2 + j], dev)

    def gather_far():
        arrive(bt.at[0, shard(2), FIRST_A], ag.at[0, 4])
        arrive(bt.at[0, shard(2), FIRST_B], ag.at[0, 5])
        for dev, q in ((yp, 1), (ym, 2)):
            send(bt.at[0, shard(2), FIRST], bt.at[q, shard(2), FIRST], ag.at[q, 4], dev)

    def take_rest(q):
        dev = yp if q % 2 == 1 else ym
        arrive(bt.at[q, shard(0), REST], ag.at[q, 0])
        if q < 5:
            send(bt.at[q, shard(0), REST], bt.at[q + 2, shard(0), REST], ag.at[q + 2, 0], dev)
        elif q == 5:
            send(bt.at[5, shard(0), REST_A], bt.at[7, shard(0), REST_A], ag.at[7, 0], dev)
        else:
            send(bt.at[6, shard(0), REST_B], bt.at[7, shard(0), REST_B], ag.at[7, 1], dev)
        across(q, bt.at[q, shard(0)])

    def take_rest_far(source):
        if source == 5:
            arrive(bt.at[7, shard(0), REST_A], ag.at[7, 0])
            across_a(7, bt.at[7, shard(0)])
        else:
            arrive(bt.at[7, shard(0), REST_B], ag.at[7, 1])
            across_b(7, bt.at[7, shard(0)])

    def take_first(q, j):
        dev = yp if q % 2 == 1 else ym
        arrive(bt.at[q, shard(j), FIRST], ag.at[q, 2 + j])
        if q < 5:
            send(bt.at[q, shard(j), FIRST], bt.at[q + 2, shard(j), FIRST], ag.at[q + 2, 2 + j], dev)
        elif (q == 5 and j in (0, 3)) or (q == 6 and j in (1, 2)):
            send(bt.at[q, shard(j), FIRST], bt.at[7, shard(j), FIRST], ag.at[7, 2 + j], dev)

    def relay(q, j):
        if j == 3:
            arrive(bt.at[q, shard(3), REST_A], ag.at[q, 6])
            send(bt.at[q, shard(3), REST_A], bt.at[q, shard(2), REST_A], ag.at[q, 8], xp)
        else:
            arrive(bt.at[q, shard(1), REST_B], ag.at[q, 7])
            send(bt.at[q, shard(1), REST_B], bt.at[q, shard(2), REST_B], ag.at[q, 9], xm)

    def take_far(q):
        arrive(bt.at[q, shard(1), REST_A], ag.at[q, 10])
        arrive(bt.at[q, shard(3), REST_B], ag.at[q, 11])
        arrive(bt.at[q, shard(2), REST_A], ag.at[q, 8])
        arrive(bt.at[q, shard(2), REST_B], ag.at[q, 9])

    def product(q, i):
        if q == 0 and i == 0:
            load_b.wait()
        multiply(q, 1 - core if i < 2 else core, i % 2)
        if i == 1:
            swap(q)

    def multiply(q, which, i):
        start = pl.multiple_of(which * HALF + i * BLOCK, BLOCK)
        cb[q, which, :, i * BLOCK : (i + 1) * BLOCK] = lax.dot_general(
            bt[q], a[pl.ds(start, BLOCK), :], (((1,), (1,)), ((), ())), preferred_element_type=jnp.float32
        )

    def swap(q):
        send(cb.at[q, 1 - core], xb.at[q], ex.at[q], partner)

    def encode(values, ref):
        parts = [values[:, m * TILE : (m + 1) * TILE].reshape(SHARD // 8, 8, TILE) for m in range(HALF // TILE)]
        top = jnp.max(jnp.abs(parts[0]), axis=0)
        for part in parts[1:]:
            top = jnp.maximum(top, jnp.max(jnp.abs(part), axis=0))
        power = jnp.ceil(jnp.log2(jnp.maximum(top, 1e-30)))
        scale = (jnp.exp2(-power) * LEVELS)[None]
        for m, part in enumerate(parts):
            whole = jnp.round(part * scale).reshape(SHARD, TILE)
            ref[m * SHARD : (m + 1) * SHARD, :] = whole.astype(jnp.int32).astype(jnp.int16)
        both = jnp.concatenate([power, power], axis=0)
        ref[CODED - 16 :, :] = both.astype(jnp.int32).astype(jnp.int16)

    def decode(ref):
        power = ref[CODED - 16 :, :].astype(jnp.int32).astype(jnp.float32)[:8]
        step = (jnp.exp2(power) * (1.0 / LEVELS))[None]
        parts = []
        for m in range(HALF // TILE):
            whole = ref[m * SHARD : (m + 1) * SHARD, :].astype(jnp.int32).astype(jnp.float32)
            parts.append((whole.reshape(SHARD // 8, 8, TILE) * step).reshape(SHARD, TILE))
        return jnp.concatenate(parts, axis=1)

    evens, slots = [], []
    for h in range(2):
        e = (z + NZ - h) % NZ
        evens.append(e % 2)
        slots.append((e // 2 + NX - x) % NX)
    halves = [origin(q) // 4 for q in range(8)]
    parity = [evens[0] + (evens[1] - evens[0]) * h for h in halves]
    slot0 = [slots[0] + (slots[1] - slots[0]) * h for h in halves]
    plus3 = (3 * sigma + 1) // 2
    minus3 = (1 - 3 * sigma) // 2

    def at(q, steps):
        j = (slot0[q] + steps + NX) % NX
        return cb.at[q, core, pl.ds(pl.multiple_of(j * SHARD, SHARD), SHARD), :]

    base = BASE

    def is_even(q):
        return parity[q] == 0

    def pass_on(q, values, slot, sem, dev):
        encode(values, eb.at[q, sem])
        copy_of(eb.at[q, sem], rb.at[q, slot], ssem.at[base + 4 * q + sem], ch.at[q, slot], dev).start()

    def merge(q):
        arrive(xb.at[q], ex.at[q])
        cb[q, core] += xb[q]

    def add_in(q, steps, ref, sem):
        arrive(ref, sem)
        return at(q, steps)[...] + decode(ref)

    def stage1(q):
        @pl.when(is_even(q))
        def _():
            pass_on(q, at(q, 2)[...], 0, 0, ahead)

        @pl.when(jnp.logical_not(is_even(q)))
        def _():
            pass_on(q, at(q, minus3)[...], 1, 1, behind)

    def stage2(q):
        @pl.when(jnp.logical_not(is_even(q)))
        def _():
            pass_on(q, add_in(q, plus3, rb.at[q, 0], ch.at[q, 0]), 0, 0, ahead)

    def stage3(q):
        @pl.when(is_even(q))
        def _():
            for slot, steps, dev in ((1, -sigma, behind), (0, sigma, ahead)):
                pass_on(q, add_in(q, steps, rb.at[q, slot], ch.at[q, slot]), 2 + slot, 1 + slot, dev)

    up, down = (1 + sigma) // 2, (1 - sigma) // 2

    def stage4(q):
        @pl.when(jnp.logical_not(is_even(q)))
        def _():
            for slot, steps, dev in ((1, down, behind), (0, up, ahead)):
                pass_on(q, add_in(q, steps, rb.at[q, 2 + slot], ch.at[q, 2 + slot]), 2 + slot, 2 + slot, dev)

    def straight(q, values, slot, sem, dev):
        f = FAST.index(q)
        encode(values, eb.at[q, sem])
        copy_of(eb.at[q, sem], fb.at[f, slot], ssem.at[base + 4 * q + sem], fch.at[f, slot], dev).start()

    def fast1(q):
        @pl.when(is_even(q))
        def _():
            straight(q, at(q, 2)[...], 0, 0, ahead)
            straight(q, at(q, 1)[...], 3, 1, along_z(2))
            straight(q, at(q, -1)[...], 4, 2, along_z(-2))

        @pl.when(jnp.logical_not(is_even(q)))
        def _():
            straight(q, at(q, minus3)[...], 5 + up, 0, along_z(-3 * sigma))
            straight(q, at(q, 1)[...], 1, 1, along_z(1))
            straight(q, at(q, 0)[...], 2, 2, along_z(-1))

    def fast2(q):
        @pl.when(jnp.logical_not(is_even(q)))
        def _():
            f = FAST.index(q)
            straight(q, add_in(q, plus3, fb.at[f, 0], fch.at[f, 0]), 5 + down, 3, along_z(3 * sigma))

    def place(ref, index):
        columns = pl.ds(pl.multiple_of(core * HALF, HALF), HALF)
        return ref.at[index, :, columns]

    def finish(q):
        origin_y = origin(q)
        index = origin_y % 2
        mine = (origin_y // 2) % 2 == core

        @pl.when(is_even(q))
        def _():
            total = at(q, 0)[...]
            if q in FAST:
                f = FAST.index(q)
                for slot in range(1, 7):
                    arrive(fb.at[f, slot], fch.at[f, slot])
                    total += decode(fb.at[f, slot])
            else:
                for slot in (2, 3):
                    arrive(rb.at[q, slot], ch.at[q, slot])
                    total += decode(rb.at[q, slot])
            total = total.astype(jnp.bfloat16)

            @pl.when(mine)
            def _():
                place(done, index)[...] = total

            @pl.when(jnp.logical_not(mine))
            def _():
                fin[index] = total
                copy_of(fin.at[index], place(done, index), fs.at[0, index], fs.at[1, index], partner).start()

    def mask_rows(part):
        if part == 0:
            load_a.wait()

        def apply_mask(i, carry):
            rows = pl.ds(pl.multiple_of(i * TILE, TILE), TILE)
            for k in range(DEPTH // TILE):
                cols = slice(k * TILE, (k + 1) * TILE)
                a[rows, cols] = jnp.where(mask[i, k] != 0, a[rows, cols], jnp.zeros((TILE, TILE), jnp.bfloat16))
            return carry

        lax.fori_loop(4 * part, 4 * part + 4, apply_mask, 0)

    for step, *args in (
        (own_rest_y,),
        (own_first_x,),
        (own_rest_x,),
        (own_first_y,),
        (gather, 3),
        (gather, 1),
        (take_rest, 1),
        (relay, 0, 3),
        (relay, 0, 1),
        (mask_rows, 0),
        (take_rest, 2),
        (gather_far,),
        (mask_rows, 1),
        (relay, 1, 1),
        (take_first, 1, 3),
        (take_first, 2, 1),
        (relay, 1, 3),
        (take_first, 2, 0),
        (take_first, 1, 1),
        (take_far, 0),
        (take_first, 2, 3),
        (product, 0, 0),
        (take_rest, 4),
        (relay, 2, 1),
        (relay, 2, 3),
        (take_rest, 3),
        (product, 0, 1),
        (product, 0, 2),
        (take_first, 2, 2),
        (product, 0, 3),
        (take_first, 1, 0),
        (take_far, 1),
        (take_first, 1, 2),
        (merge, 0),
        (product, 1, 0),
        (product, 1, 1),
        (product, 1, 2),
        (take_first, 4, 1),
        (relay, 4, 3),
        (stage1, 0),
        (take_first, 3, 1),
        (relay, 4, 1),
        (product, 1, 3),
        (take_first, 3, 3),
        (take_first, 4, 3),
        (merge, 1),
        (take_rest, 5),
        (stage1, 1),
        (take_first, 4, 0),
        (take_far, 2),
        (product, 2, 0),
        (product, 2, 1),
        (relay, 3, 3),
        (take_first, 3, 0),
        (relay, 3, 1),
        (take_rest, 6),
        (product, 2, 2),
        (take_first, 4, 2),
        (product, 2, 3),
        (merge, 2),
        (take_far, 4),
        (product, 4, 0),
        (stage1, 2),
        (product, 4, 1),
        (relay, 5, 1),
        (take_first, 6, 1),
        (take_first, 3, 2),
        (relay, 5, 3),
        (product, 4, 2),
        (take_rest_far, 5),
        (product, 4, 3),
        (merge, 4),
        (take_far, 3),
        (stage2, 1),
        (product, 3, 0),
        (take_rest_far, 6),
        (product, 3, 1),
        (relay, 6, 3),
        (relay, 6, 1),
        (product, 3, 2),
        (take_first, 6, 0),
        (take_first, 5, 3),
        (stage1, 4),
        (product, 3, 3),
        (merge, 3),
        (take_first, 7, 1),
        (take_far, 5),
        (stage1, 3),
        (take_first, 5, 0),
        (take_first, 5, 2),
        (take_first, 5, 1),
        (product, 5, 0),
        (stage2, 2),
        (product, 5, 1),
        (stage2, 0),
        (product, 5, 2),
        (relay, 7, 3),
        (relay, 7, 1),
        (product, 5, 3),
        (take_first, 6, 2),
        (merge, 5),
        (stage1, 5),
        (stage3, 1),
        (take_first, 6, 3),
        (take_far, 6),
        (product, 6, 0),
        (product, 6, 1),
        (product, 6, 2),
        (take_first, 7, 0),
        (stage2, 4),
        (stage2, 3),
        (take_first, 7, 3),
        (stage3, 2),
        (product, 6, 3),
        (stage3, 0),
        (merge, 6),
        (stage2, 5),
        (take_far, 7),
        (fast1, 6),
        (take_first, 7, 2),
        (product, 7, 0),
        (product, 7, 1),
        (product, 7, 2),
        (stage3, 4),
        (stage3, 3),
        (product, 7, 3),
        (merge, 7),
        (fast1, 7),
        (stage4, 1),
        (stage3, 5),
        (fast2, 6),
        (fast2, 7),
        (stage4, 0),
        (stage4, 3),
        (stage4, 4),
        (stage4, 2),
        (finish, 1),
        (stage4, 5),
        (finish, 6),
        (finish, 4),
        (finish, 3),
        (finish, 2),
        (finish, 0),
        (finish, 5),
        (finish, 7),
    ):
        step(*args)

    for index in range(2):
        half = pl.ds(pl.multiple_of((1 - core) * HALF, HALF), HALF)
        arrive(done.at[index, :, half], fs.at[1, index])
        copy_of(fin.at[index], place(done, index), fs.at[0, index], fs.at[1, index], partner).wait_send()
    for index in range(2):
        out[index * SHARD : (index + 1) * SHARD, :] = done[index]

    for copy in pending:
        copy.wait_send()
    for q in range(8):
        @pl.when(is_even(q))
        def _():
            for slot in range(3):
                copy_of(rb.at[q, 0], rb.at[q, 0], ssem.at[base + 4 * q + slot], ch.at[q, 0], partner).wait_send()

        @pl.when(jnp.logical_not(is_even(q)))
        def _():
            for slot in range(4):
                copy_of(rb.at[q, 0], rb.at[q, 0], ssem.at[base + 4 * q + slot], ch.at[q, 0], partner).wait_send()


def per_device(amplitudes, integrals, tile_mask):
    result = pl.pallas_call(
        kernel,
        out_shape=jax.ShapeDtypeStruct((2 * SHARD, ROWS), jnp.bfloat16),
        in_specs=[
            pl.BlockSpec(memory_space=pl.ANY),
            pl.BlockSpec(memory_space=pl.ANY),
            pl.BlockSpec(memory_space=pltpu.SMEM),
        ],
        out_specs=pl.BlockSpec(memory_space=pltpu.VMEM),
        scratch_shapes=[
            pltpu.VMEM((ROWS, DEPTH), jnp.bfloat16),
            pltpu.VMEM((8, 4 * SHARD, DEPTH), jnp.bfloat16),
            pltpu.VMEM((8, 2, 4 * SHARD, HALF), jnp.float32),
            pltpu.VMEM((8, 4 * SHARD, HALF), jnp.float32),
            pltpu.VMEM((8, 4, CODED, TILE), jnp.int16),
            pltpu.VMEM((8, 4, CODED, TILE), jnp.int16),
            pltpu.VMEM((len(FAST), 7, CODED, TILE), jnp.int16),
            pltpu.VMEM((2, SHARD, HALF), jnp.bfloat16),
            pltpu.VMEM((2, SHARD, ROWS), jnp.bfloat16),
            pltpu.SemaphoreType.DMA((2,)),
            pltpu.SemaphoreType.DMA((N_SEND,)),
            pltpu.SemaphoreType.DMA((8, 12)),
            pltpu.SemaphoreType.DMA((8,)),
            pltpu.SemaphoreType.DMA((8, 4)),
            pltpu.SemaphoreType.DMA((len(FAST), 7)),
            pltpu.SemaphoreType.DMA((2, 2)),
        ],
        compiler_params=pltpu.CompilerParams(
            collective_id=0, has_side_effects=True, vmem_limit_bytes=60 * 1024 * 1024
        ),
    )(amplitudes, integrals.T, tile_mask)
    return result.T


def solution(mesh):
    placed = (P("row", "col"), P("col", "row"), P("row", "col"))
    return jax.shard_map(
        per_device, mesh=mesh, in_specs=placed, out_specs=P("row", "col"), check_vma=False
    )
```

```python
import jax
import jax.numpy as jnp
from jax import lax
from jax.experimental import pallas as pl
from jax.experimental.pallas import tpu as pltpu
from jax.sharding import PartitionSpec as P

MESH = pl.DeviceIdType.MESH
NX, NY, NZ = 4, 8, 8
TILE = 128
SHARD = 32
ROWS = 1024
DEPTH = 2048
HALF = ROWS // 2
LEVELS = 32000.0
CODED = SHARD * HALF // TILE + 16
BLOCK = 256
SPLIT = 768

FIRST = slice(0, SPLIT)
REST = slice(SPLIT, DEPTH)
FIRST_A = slice(0, SPLIT // 2)
FIRST_B = slice(SPLIT // 2, SPLIT)
REST_A = slice(SPLIT, (SPLIT + DEPTH) // 2)
REST_B = slice((SPLIT + DEPTH) // 2, DEPTH)
BASE = 100
N_SEND = BASE + 32
FAST = (7,)


def shard(j):
    return slice(j * SHARD, (j + 1) * SHARD)


def kernel(a_hbm, own, mask, out, a, bt, cb, xb, eb, rb, fb, fin, done, lsem, ssem, ag, ex, ch, fch, fs):
    row, col = lax.axis_index("row"), lax.axis_index("col")
    x, y = row // NY, row % NY
    z, core = col // 2, col % 2
    xp = (((x + 1) % NX) * NY + y, col)
    xm = (((x + NX - 1) % NX) * NY + y, col)
    yp = (x * NY + (y + 1) % NY, col)
    ym = (x * NY + (y + NY - 1) % NY, col)
    sigma = 1 - 2 * core
    ahead = (row, ((z + NZ + sigma) % NZ) * 2 + core)
    behind = (row, ((z + NZ - sigma) % NZ) * 2 + core)
    partner = (row, z * 2 + 1 - core)

    def along_z(delta):
        return (row, ((z + NZ + delta) % NZ) * 2 + core)


    load_a = pltpu.make_async_copy(a_hbm, a, lsem.at[0])
    load_b = pltpu.make_async_copy(own, bt.at[0, shard(0)], lsem.at[1])
    load_a.start()
    load_b.start()

    barrier = pltpu.get_barrier_semaphore()
    for dev in [xp, xm, yp, ym, partner] + [along_z(d) for d in (1, -1, 2, -2, 3, -3)]:
        pl.semaphore_signal(barrier, inc=1, device_id=dev, device_id_type=MESH)
    pl.semaphore_wait(barrier, 11)

    pending = []
    count = [0]

    def copy_of(src, dst, send_sem, recv_sem, dev):
        return pltpu.make_async_remote_copy(
            src_ref=src, dst_ref=dst, send_sem=send_sem, recv_sem=recv_sem, device_id=dev, device_id_type=MESH
        )

    def send(src, dst, recv_sem, dev):
        copy = copy_of(src, dst, ssem.at[count[0]], recv_sem, dev)
        count[0] += 1
        copy.start()
        pending.append(copy)

    def arrive(dst, recv_sem):
        copy_of(dst, dst, ssem.at[0], recv_sem, partner).wait_recv()

    def origin(q):
        step = (q + 1) // 2
        return (y + NY - step) % NY if q % 2 == 1 else (y + step) % NY

    def own_first_x():
        for dev, j, k in ((xp, 3, 2), (xm, 1, 3)):
            send(own.at[:, FIRST], bt.at[0, shard(j), FIRST], ag.at[0, k], dev)

    def own_rest_y():
        for dev, q in ((yp, 1), (ym, 2)):
            send(own.at[:, REST], bt.at[q, shard(0), REST], ag.at[q, 0], dev)

    def own_first_y():
        for dev, q in ((yp, 1), (ym, 2)):
            send(own.at[:, FIRST], bt.at[q, shard(0), FIRST], ag.at[q, 2], dev)

    def across_a(q, src):
        send(src.at[:, REST_A], bt.at[q, shard(3), REST_A], ag.at[q, 6], xp)
        send(src.at[:, REST_A], bt.at[q, shard(1), REST_A], ag.at[q, 10], xm)

    def across_b(q, src):
        send(src.at[:, REST_B], bt.at[q, shard(1), REST_B], ag.at[q, 7], xm)
        send(src.at[:, REST_B], bt.at[q, shard(3), REST_B], ag.at[q, 11], xp)

    def across(q, src):
        send(src.at[:, REST_A], bt.at[q, shard(3), REST_A], ag.at[q, 6], xp)
        send(src.at[:, REST_B], bt.at[q, shard(1), REST_B], ag.at[q, 7], xm)
        send(src.at[:, REST_B], bt.at[q, shard(3), REST_B], ag.at[q, 11], xp)
        send(src.at[:, REST_A], bt.at[q, shard(1), REST_A], ag.at[q, 10], xm)

    def own_rest_x():
        across(0, own)

    def gather(j):
        dev, half, k = (xp, FIRST_A, 4) if j == 3 else (xm, FIRST_B, 5)
        arrive(bt.at[0, shard(j), FIRST], ag.at[0, 2 if j == 3 else 3])
        send(bt.at[0, shard(j), half], bt.at[0, shard(2), half], ag.at[0, k], dev)
        for dev, q in ((yp, 1), (ym, 2)):
            send(bt.at[0, shard(j), FIRST], bt.at[q, shard(j), FIRST], ag.at[q, 2 + j], dev)

    def gather_far():
        arrive(bt.at[0, shard(2), FIRST_A], ag.at[0, 4])
        arrive(bt.at[0, shard(2), FIRST_B], ag.at[0, 5])
        for dev, q in ((yp, 1), (ym, 2)):
            send(bt.at[0, shard(2), FIRST], bt.at[q, shard(2), FIRST], ag.at[q, 4], dev)

    def take_rest(q):
        dev = yp if q % 2 == 1 else ym
        arrive(bt.at[q, shard(0), REST], ag.at[q, 0])
        if q < 5:
            send(bt.at[q, shard(0), REST], bt.at[q + 2, shard(0), REST], ag.at[q + 2, 0], dev)
        elif q == 5:
            send(bt.at[5, shard(0), REST_A], bt.at[7, shard(0), REST_A], ag.at[7, 0], dev)
        else:
            send(bt.at[6, shard(0), REST_B], bt.at[7, shard(0), REST_B], ag.at[7, 1], dev)
        across(q, bt.at[q, shard(0)])

    def take_rest_far(source):
        if source == 5:
            arrive(bt.at[7, shard(0), REST_A], ag.at[7, 0])
            across_a(7, bt.at[7, shard(0)])
        else:
            arrive(bt.at[7, shard(0), REST_B], ag.at[7, 1])
            across_b(7, bt.at[7, shard(0)])

    def take_first(q, j):
        dev = yp if q % 2 == 1 else ym
        arrive(bt.at[q, shard(j), FIRST], ag.at[q, 2 + j])
        if q < 5:
            send(bt.at[q, shard(j), FIRST], bt.at[q + 2, shard(j), FIRST], ag.at[q + 2, 2 + j], dev)
        elif (q == 5 and j in (0, 3)) or (q == 6 and j in (1, 2)):
            send(bt.at[q, shard(j), FIRST], bt.at[7, shard(j), FIRST], ag.at[7, 2 + j], dev)

    def relay(q, j):
        if j == 3:
            arrive(bt.at[q, shard(3), REST_A], ag.at[q, 6])
            send(bt.at[q, shard(3), REST_A], bt.at[q, shard(2), REST_A], ag.at[q, 8], xp)
        else:
            arrive(bt.at[q, shard(1), REST_B], ag.at[q, 7])
            send(bt.at[q, shard(1), REST_B], bt.at[q, shard(2), REST_B], ag.at[q, 9], xm)

    def take_far(q):
        arrive(bt.at[q, shard(1), REST_A], ag.at[q, 10])
        arrive(bt.at[q, shard(3), REST_B], ag.at[q, 11])
        arrive(bt.at[q, shard(2), REST_A], ag.at[q, 8])
        arrive(bt.at[q, shard(2), REST_B], ag.at[q, 9])

    def product(q, i):
        if q == 0 and i == 0:
            load_b.wait()
        multiply(q, 1 - core if i < 2 else core, i % 2)
        if i == 1:
            for row_slot in (q,) if q in (0, 7) else (q, q + 1):
                swap(row_slot)

    def multiply(q, which, i):
        start = pl.multiple_of(which * HALF + i * BLOCK, BLOCK)
        n = 1 if q in (0, 7) else 2
        sums = lax.dot_general(
            bt[q : q + n].reshape(n * 4 * SHARD, DEPTH),
            a[pl.ds(start, BLOCK), :],
            (((1,), (1,)), ((), ())),
            preferred_element_type=jnp.float32,
        )
        for r in range(n):
            cb[q + r, which, :, i * BLOCK : (i + 1) * BLOCK] = sums[r * 4 * SHARD : (r + 1) * 4 * SHARD]

    def swap(q):
        send(cb.at[q, 1 - core], xb.at[q], ex.at[q], partner)

    def encode(values, ref):
        parts = [values[:, m * TILE : (m + 1) * TILE].reshape(SHARD // 8, 8, TILE) for m in range(HALF // TILE)]
        top = jnp.max(jnp.abs(parts[0]), axis=0)
        for part in parts[1:]:
            top = jnp.maximum(top, jnp.max(jnp.abs(part), axis=0))
        power = jnp.ceil(jnp.log2(jnp.maximum(top, 1e-30)))
        scale = (jnp.exp2(-power) * LEVELS)[None]
        for m, part in enumerate(parts):
            whole = jnp.round(part * scale).reshape(SHARD, TILE)
            ref[m * SHARD : (m + 1) * SHARD, :] = whole.astype(jnp.int32).astype(jnp.int16)
        both = jnp.concatenate([power, power], axis=0)
        ref[CODED - 16 :, :] = both.astype(jnp.int32).astype(jnp.int16)

    def decode(ref):
        power = ref[CODED - 16 :, :].astype(jnp.int32).astype(jnp.float32)[:8]
        step = (jnp.exp2(power) * (1.0 / LEVELS))[None]
        parts = []
        for m in range(HALF // TILE):
            whole = ref[m * SHARD : (m + 1) * SHARD, :].astype(jnp.int32).astype(jnp.float32)
            parts.append((whole.reshape(SHARD // 8, 8, TILE) * step).reshape(SHARD, TILE))
        return jnp.concatenate(parts, axis=1)

    evens, slots = [], []
    for h in range(2):
        e = (z + NZ - h) % NZ
        evens.append(e % 2)
        slots.append((e // 2 + NX - x) % NX)
    halves = [origin(q) // 4 for q in range(8)]
    parity = [evens[0] + (evens[1] - evens[0]) * h for h in halves]
    slot0 = [slots[0] + (slots[1] - slots[0]) * h for h in halves]
    plus3 = (3 * sigma + 1) // 2
    minus3 = (1 - 3 * sigma) // 2

    def at(q, steps):
        j = (slot0[q] + steps + NX) % NX
        return cb.at[q, core, pl.ds(pl.multiple_of(j * SHARD, SHARD), SHARD), :]

    base = BASE

    def is_even(q):
        return parity[q] == 0

    def pass_on(q, values, slot, sem, dev):
        encode(values, eb.at[q, sem])
        copy_of(eb.at[q, sem], rb.at[q, slot], ssem.at[base + 4 * q + sem], ch.at[q, slot], dev).start()

    def merge(q):
        arrive(xb.at[q], ex.at[q])
        cb[q, core] += xb[q]

    def add_in(q, steps, ref, sem):
        arrive(ref, sem)
        return at(q, steps)[...] + decode(ref)

    def stage1(q):
        @pl.when(is_even(q))
        def _():
            pass_on(q, at(q, 2)[...], 0, 0, ahead)

        @pl.when(jnp.logical_not(is_even(q)))
        def _():
            pass_on(q, at(q, minus3)[...], 1, 1, behind)

    def stage2(q):
        @pl.when(jnp.logical_not(is_even(q)))
        def _():
            pass_on(q, add_in(q, plus3, rb.at[q, 0], ch.at[q, 0]), 0, 0, ahead)

    def stage3(q):
        @pl.when(is_even(q))
        def _():
            for slot, steps, dev in ((1, -sigma, behind), (0, sigma, ahead)):
                pass_on(q, add_in(q, steps, rb.at[q, slot], ch.at[q, slot]), 2 + slot, 1 + slot, dev)

    up, down = (1 + sigma) // 2, (1 - sigma) // 2

    def stage4(q):
        @pl.when(jnp.logical_not(is_even(q)))
        def _():
            for slot, steps, dev in ((1, down, behind), (0, up, ahead)):
                pass_on(q, add_in(q, steps, rb.at[q, 2 + slot], ch.at[q, 2 + slot]), 2 + slot, 2 + slot, dev)

    def straight(q, values, slot, sem, dev):
        f = FAST.index(q)
        encode(values, eb.at[q, sem])
        copy_of(eb.at[q, sem], fb.at[f, slot], ssem.at[base + 4 * q + sem], fch.at[f, slot], dev).start()

    def fast1(q):
        @pl.when(is_even(q))
        def _():
            straight(q, at(q, 2)[...], 0, 0, ahead)
            straight(q, at(q, 1)[...], 3, 1, along_z(2))
            straight(q, at(q, -1)[...], 4, 2, along_z(-2))

        @pl.when(jnp.logical_not(is_even(q)))
        def _():
            straight(q, at(q, minus3)[...], 5 + up, 0, along_z(-3 * sigma))
            straight(q, at(q, 1)[...], 1, 1, along_z(1))
            straight(q, at(q, 0)[...], 2, 2, along_z(-1))

    def fast2(q):
        @pl.when(jnp.logical_not(is_even(q)))
        def _():
            f = FAST.index(q)
            straight(q, add_in(q, plus3, fb.at[f, 0], fch.at[f, 0]), 5 + down, 3, along_z(3 * sigma))

    def place(ref, index):
        columns = pl.ds(pl.multiple_of(core * HALF, HALF), HALF)
        return ref.at[index, :, columns]

    def finish(q):
        origin_y = origin(q)
        index = origin_y % 2
        mine = (origin_y // 2) % 2 == core

        @pl.when(is_even(q))
        def _():
            total = at(q, 0)[...]
            if q in FAST:
                f = FAST.index(q)
                for slot in range(1, 7):
                    arrive(fb.at[f, slot], fch.at[f, slot])
                    total += decode(fb.at[f, slot])
            else:
                for slot in (2, 3):
                    arrive(rb.at[q, slot], ch.at[q, slot])
                    total += decode(rb.at[q, slot])
            total = total.astype(jnp.bfloat16)

            @pl.when(mine)
            def _():
                place(done, index)[...] = total

            @pl.when(jnp.logical_not(mine))
            def _():
                fin[index] = total
                copy_of(fin.at[index], place(done, index), fs.at[0, index], fs.at[1, index], partner).start()

    def mask_rows(part):
        if part == 0:
            load_a.wait()

        def apply_mask(i, carry):
            rows = pl.ds(pl.multiple_of(i * TILE, TILE), TILE)
            for k in range(DEPTH // TILE):
                cols = slice(k * TILE, (k + 1) * TILE)
                a[rows, cols] = jnp.where(mask[i, k] != 0, a[rows, cols], jnp.zeros((TILE, TILE), jnp.bfloat16))
            return carry

        lax.fori_loop(4 * part, 4 * part + 4, apply_mask, 0)

    for step, *args in (
        (own_rest_y,),
        (own_rest_x,),
        (mask_rows, 0),
        (own_first_y,),
        (own_first_x,),
        (relay, 0, 3),
        (relay, 0, 1),
        (take_rest, 2),
        (take_rest, 1),
        (gather, 1),
        (gather, 3),
        (relay, 2, 3),
        (take_first, 1, 0),
        (relay, 2, 1),
        (take_rest, 4),
        (take_rest, 3),
        (take_far, 0),
        (take_first, 2, 1),
        (mask_rows, 1),
        (gather_far,),
        (product, 0, 0),
        (take_first, 1, 1),
        (take_first, 2, 3),
        (product, 0, 1),
        (relay, 1, 1),
        (take_first, 2, 0),
        (take_far, 2),
        (relay, 1, 3),
        (take_first, 1, 3),
        (product, 0, 2),
        (relay, 4, 1),
        (relay, 4, 3),
        (product, 0, 3),
        (take_rest, 5),
        (relay, 3, 3),
        (merge, 0),
        (relay, 3, 1),
        (take_rest, 6),
        (take_first, 1, 2),
        (stage1, 0),
        (take_first, 2, 2),
        (take_first, 4, 1),
        (take_first, 3, 1),
        (take_far, 1),
        (product, 1, 0),
        (product, 1, 1),
        (take_first, 3, 3),
        (take_first, 4, 3),
        (product, 1, 2),
        (take_first, 4, 0),
        (take_first, 3, 0),
        (product, 1, 3),
        (merge, 1),
        (take_rest_far, 5),
        (stage1, 1),
        (merge, 2),
        (stage2, 0),
        (take_far, 4),
        (relay, 5, 1),
        (take_first, 4, 2),
        (relay, 5, 3),
        (stage1, 2),
        (take_far, 3),
        (take_first, 3, 2),
        (product, 3, 0),
        (relay, 6, 3),
        (relay, 6, 1),
        (product, 3, 1),
        (take_rest_far, 6),
        (product, 3, 2),
        (take_first, 5, 3),
        (product, 3, 3),
        (merge, 3),
        (stage2, 1),
        (take_first, 6, 1),
        (merge, 4),
        (stage3, 0),
        (take_first, 5, 0),
        (take_far, 5),
        (take_first, 6, 0),
        (stage1, 4),
        (stage1, 3),
        (take_first, 5, 2),
        (take_first, 6, 2),
        (stage2, 2),
        (take_far, 6),
        (take_first, 5, 1),
        (take_first, 6, 3),
        (product, 5, 0),
        (product, 5, 1),
        (relay, 7, 3),
        (relay, 7, 1),
        (product, 5, 2),
        (product, 5, 3),
        (merge, 5),
        (stage1, 5),
        (merge, 6),
        (stage3, 1),
        (stage1, 6),
        (stage4, 0),
        (take_first, 7, 0),
        (take_first, 7, 1),
        (take_first, 7, 2),
        (stage2, 3),
        (stage2, 4),
        (take_first, 7, 3),
        (stage3, 2),
        (take_far, 7),
        (product, 7, 0),
        (product, 7, 1),
        (product, 7, 2),
        (stage2, 5),
        (product, 7, 3),
        (stage2, 6),
        (merge, 7),
        (fast1, 7),
        (stage3, 4),
        (stage3, 3),
        (stage3, 5),
        (stage3, 6),
        (fast2, 7),
        (stage4, 2),
        (stage4, 1),
        (stage4, 4),
        (stage4, 3),
        (stage4, 5),
        (stage4, 6),
        (finish, 2),
        (finish, 0),
        (finish, 1),
        (finish, 4),
        (finish, 3),
        (finish, 7),
        (finish, 5),
        (finish, 6),
    ):
        step(*args)

    for index in range(2):
        half = pl.ds(pl.multiple_of((1 - core) * HALF, HALF), HALF)
        arrive(done.at[index, :, half], fs.at[1, index])
        copy_of(fin.at[index], place(done, index), fs.at[0, index], fs.at[1, index], partner).wait_send()
    for index in range(2):
        out[index * SHARD : (index + 1) * SHARD, :] = done[index]

    for copy in pending:
        copy.wait_send()
    for q in range(8):
        @pl.when(is_even(q))
        def _():
            for slot in range(3):
                copy_of(rb.at[q, 0], rb.at[q, 0], ssem.at[base + 4 * q + slot], ch.at[q, 0], partner).wait_send()

        @pl.when(jnp.logical_not(is_even(q)))
        def _():
            for slot in range(4):
                copy_of(rb.at[q, 0], rb.at[q, 0], ssem.at[base + 4 * q + slot], ch.at[q, 0], partner).wait_send()


def per_device(amplitudes, integrals, tile_mask):
    result = pl.pallas_call(
        kernel,
        out_shape=jax.ShapeDtypeStruct((2 * SHARD, ROWS), jnp.bfloat16),
        in_specs=[
            pl.BlockSpec(memory_space=pl.ANY),
            pl.BlockSpec(memory_space=pl.ANY),
            pl.BlockSpec(memory_space=pltpu.SMEM),
        ],
        out_specs=pl.BlockSpec(memory_space=pltpu.VMEM),
        scratch_shapes=[
            pltpu.VMEM((ROWS, DEPTH), jnp.bfloat16),
            pltpu.VMEM((8, 4 * SHARD, DEPTH), jnp.bfloat16),
            pltpu.VMEM((8, 2, 4 * SHARD, HALF), jnp.float32),
            pltpu.VMEM((8, 4 * SHARD, HALF), jnp.float32),
            pltpu.VMEM((8, 4, CODED, TILE), jnp.int16),
            pltpu.VMEM((8, 4, CODED, TILE), jnp.int16),
            pltpu.VMEM((len(FAST), 7, CODED, TILE), jnp.int16),
            pltpu.VMEM((2, SHARD, HALF), jnp.bfloat16),
            pltpu.VMEM((2, SHARD, ROWS), jnp.bfloat16),
            pltpu.SemaphoreType.DMA((2,)),
            pltpu.SemaphoreType.DMA((N_SEND,)),
            pltpu.SemaphoreType.DMA((8, 12)),
            pltpu.SemaphoreType.DMA((8,)),
            pltpu.SemaphoreType.DMA((8, 4)),
            pltpu.SemaphoreType.DMA((len(FAST), 7)),
            pltpu.SemaphoreType.DMA((2, 2)),
        ],
        compiler_params=pltpu.CompilerParams(
            collective_id=0, has_side_effects=True, vmem_limit_bytes=60 * 1024 * 1024
        ),
    )(amplitudes, integrals.T, tile_mask)
    return result.T


def solution(mesh):
    placed = (P("row", "col"), P("col", "row"), P("row", "col"))
    return jax.shard_map(
        per_device, mesh=mesh, in_specs=placed, out_specs=P("row", "col"), check_vma=False
    )
```

```python
import jax
import jax.numpy as jnp
from jax import lax
from jax.experimental import pallas as pl
from jax.experimental.pallas import tpu as pltpu
from jax.sharding import PartitionSpec as P

MESH = pl.DeviceIdType.MESH
NX, NY, NZ = 4, 8, 8
TILE = 128
SHARD = 32
ROWS = 1024
DEPTH = 2048
HALF = ROWS // 2
LEVELS = 32000.0
CODED = SHARD * HALF // TILE + 16
BLOCK = 256
SPLIT = 768

FIRST = slice(0, SPLIT)
REST = slice(SPLIT, DEPTH)
FIRST_A = slice(0, SPLIT // 2)
FIRST_B = slice(SPLIT // 2, SPLIT)
REST_A = slice(SPLIT, (SPLIT + DEPTH) // 2)
REST_B = slice((SPLIT + DEPTH) // 2, DEPTH)
BASE = 100
N_SEND = BASE + 32
FAST = (7,)


def shard(j):
    return slice(j * SHARD, (j + 1) * SHARD)


def kernel(a_hbm, own, mask, out, a, bt, cb, xb, eb, rb, fb, fin, done, lsem, ssem, ag, ex, ch, fch, fs):
    row, col = lax.axis_index("row"), lax.axis_index("col")
    x, y = row // NY, row % NY
    z, core = col // 2, col % 2
    xp = (((x + 1) % NX) * NY + y, col)
    xm = (((x + NX - 1) % NX) * NY + y, col)
    yp = (x * NY + (y + 1) % NY, col)
    ym = (x * NY + (y + NY - 1) % NY, col)
    sigma = 1 - 2 * core
    ahead = (row, ((z + NZ + sigma) % NZ) * 2 + core)
    behind = (row, ((z + NZ - sigma) % NZ) * 2 + core)
    partner = (row, z * 2 + 1 - core)

    def along_z(delta):
        return (row, ((z + NZ + delta) % NZ) * 2 + core)


    load_a = pltpu.make_async_copy(a_hbm, a, lsem.at[0])
    load_b = pltpu.make_async_copy(own, bt.at[0, shard(0)], lsem.at[1])
    load_a.start()
    load_b.start()

    barrier = pltpu.get_barrier_semaphore()
    for dev in [xp, xm, yp, ym, partner] + [along_z(d) for d in (1, -1, 2, -2, 3, -3)]:
        pl.semaphore_signal(barrier, inc=1, device_id=dev, device_id_type=MESH)
    pl.semaphore_wait(barrier, 11)

    pending = []
    count = [0]

    def copy_of(src, dst, send_sem, recv_sem, dev):
        return pltpu.make_async_remote_copy(
            src_ref=src, dst_ref=dst, send_sem=send_sem, recv_sem=recv_sem, device_id=dev, device_id_type=MESH
        )

    def send(src, dst, recv_sem, dev):
        copy = copy_of(src, dst, ssem.at[count[0]], recv_sem, dev)
        count[0] += 1
        copy.start()
        pending.append(copy)

    def arrive(dst, recv_sem):
        copy_of(dst, dst, ssem.at[0], recv_sem, partner).wait_recv()

    def origin(q):
        step = (q + 1) // 2
        return (y + NY - step) % NY if q % 2 == 1 else (y + step) % NY

    def own_first_x():
        for dev, j, k in ((xp, 3, 2), (xm, 1, 3)):
            send(own.at[:, FIRST], bt.at[0, shard(j), FIRST], ag.at[0, k], dev)

    def own_rest_y():
        for dev, q in ((yp, 1), (ym, 2)):
            send(own.at[:, REST], bt.at[q, shard(0), REST], ag.at[q, 0], dev)

    def own_first_y():
        for dev, q in ((yp, 1), (ym, 2)):
            send(own.at[:, FIRST], bt.at[q, shard(0), FIRST], ag.at[q, 2], dev)

    def across_a(q, src):
        send(src.at[:, REST_A], bt.at[q, shard(3), REST_A], ag.at[q, 6], xp)
        send(src.at[:, REST_A], bt.at[q, shard(1), REST_A], ag.at[q, 10], xm)

    def across_b(q, src):
        send(src.at[:, REST_B], bt.at[q, shard(1), REST_B], ag.at[q, 7], xm)
        send(src.at[:, REST_B], bt.at[q, shard(3), REST_B], ag.at[q, 11], xp)

    def across(q, src):
        send(src.at[:, REST_A], bt.at[q, shard(3), REST_A], ag.at[q, 6], xp)
        send(src.at[:, REST_B], bt.at[q, shard(1), REST_B], ag.at[q, 7], xm)
        send(src.at[:, REST_B], bt.at[q, shard(3), REST_B], ag.at[q, 11], xp)
        send(src.at[:, REST_A], bt.at[q, shard(1), REST_A], ag.at[q, 10], xm)

    def own_rest_x():
        across(0, own)

    def gather(j):
        dev, half, k = (xp, FIRST_A, 4) if j == 3 else (xm, FIRST_B, 5)
        arrive(bt.at[0, shard(j), FIRST], ag.at[0, 2 if j == 3 else 3])
        send(bt.at[0, shard(j), half], bt.at[0, shard(2), half], ag.at[0, k], dev)
        for dev, q in ((yp, 1), (ym, 2)):
            send(bt.at[0, shard(j), FIRST], bt.at[q, shard(j), FIRST], ag.at[q, 2 + j], dev)

    def gather_far():
        arrive(bt.at[0, shard(2), FIRST_A], ag.at[0, 4])
        arrive(bt.at[0, shard(2), FIRST_B], ag.at[0, 5])
        for dev, q in ((yp, 1), (ym, 2)):
            send(bt.at[0, shard(2), FIRST], bt.at[q, shard(2), FIRST], ag.at[q, 4], dev)

    def take_rest(q):
        dev = yp if q % 2 == 1 else ym
        arrive(bt.at[q, shard(0), REST], ag.at[q, 0])
        if q < 5:
            send(bt.at[q, shard(0), REST], bt.at[q + 2, shard(0), REST], ag.at[q + 2, 0], dev)
        elif q == 5:
            send(bt.at[5, shard(0), REST_A], bt.at[7, shard(0), REST_A], ag.at[7, 0], dev)
        else:
            send(bt.at[6, shard(0), REST_B], bt.at[7, shard(0), REST_B], ag.at[7, 1], dev)
        across(q, bt.at[q, shard(0)])

    def take_rest_far(source):
        if source == 5:
            arrive(bt.at[7, shard(0), REST_A], ag.at[7, 0])
            across_a(7, bt.at[7, shard(0)])
        else:
            arrive(bt.at[7, shard(0), REST_B], ag.at[7, 1])
            across_b(7, bt.at[7, shard(0)])

    def take_first(q, j):
        dev = yp if q % 2 == 1 else ym
        arrive(bt.at[q, shard(j), FIRST], ag.at[q, 2 + j])
        if q < 5:
            send(bt.at[q, shard(j), FIRST], bt.at[q + 2, shard(j), FIRST], ag.at[q + 2, 2 + j], dev)
        elif (q == 5 and j in (0, 3)) or (q == 6 and j in (1, 2)):
            send(bt.at[q, shard(j), FIRST], bt.at[7, shard(j), FIRST], ag.at[7, 2 + j], dev)

    def relay(q, j):
        if j == 3:
            arrive(bt.at[q, shard(3), REST_A], ag.at[q, 6])
            send(bt.at[q, shard(3), REST_A], bt.at[q, shard(2), REST_A], ag.at[q, 8], xp)
        else:
            arrive(bt.at[q, shard(1), REST_B], ag.at[q, 7])
            send(bt.at[q, shard(1), REST_B], bt.at[q, shard(2), REST_B], ag.at[q, 9], xm)

    def take_far(q):
        arrive(bt.at[q, shard(1), REST_A], ag.at[q, 10])
        arrive(bt.at[q, shard(3), REST_B], ag.at[q, 11])
        arrive(bt.at[q, shard(2), REST_A], ag.at[q, 8])
        arrive(bt.at[q, shard(2), REST_B], ag.at[q, 9])

    def product(q, i):
        if q == 0 and i == 0:
            load_b.wait()
        multiply(q, 1 - core if i < 2 else core, i % 2)
        if i == 1:
            for row_slot in (q,) if q in (0, 7) else (q, q + 1):
                swap(row_slot)

    def multiply(q, which, i):
        start = pl.multiple_of(which * HALF + i * BLOCK, BLOCK)
        n = 1 if q in (0, 7) else 2
        sums = lax.dot_general(
            bt[q : q + n].reshape(n * 4 * SHARD, DEPTH),
            a[pl.ds(start, BLOCK), :],
            (((1,), (1,)), ((), ())),
            preferred_element_type=jnp.float32,
        )
        for r in range(n):
            cb[q + r, which, :, i * BLOCK : (i + 1) * BLOCK] = sums[r * 4 * SHARD : (r + 1) * 4 * SHARD]

    def swap(q):
        send(cb.at[q, 1 - core], xb.at[q], ex.at[q], partner)

    def encode(values, ref):
        parts = [values[:, m * TILE : (m + 1) * TILE].reshape(SHARD // 8, 8, TILE) for m in range(HALF // TILE)]
        top = jnp.max(jnp.abs(parts[0]), axis=0)
        for part in parts[1:]:
            top = jnp.maximum(top, jnp.max(jnp.abs(part), axis=0))
        power = jnp.ceil(jnp.log2(jnp.maximum(top, 1e-30)))
        scale = (jnp.exp2(-power) * LEVELS)[None]
        for m, part in enumerate(parts):
            whole = jnp.round(part * scale).reshape(SHARD, TILE)
            ref[m * SHARD : (m + 1) * SHARD, :] = whole.astype(jnp.int32).astype(jnp.int16)
        both = jnp.concatenate([power, power], axis=0)
        ref[CODED - 16 :, :] = both.astype(jnp.int32).astype(jnp.int16)

    def decode(ref):
        power = ref[CODED - 16 :, :].astype(jnp.int32).astype(jnp.float32)[:8]
        step = (jnp.exp2(power) * (1.0 / LEVELS))[None]
        parts = []
        for m in range(HALF // TILE):
            whole = ref[m * SHARD : (m + 1) * SHARD, :].astype(jnp.int32).astype(jnp.float32)
            parts.append((whole.reshape(SHARD // 8, 8, TILE) * step).reshape(SHARD, TILE))
        return jnp.concatenate(parts, axis=1)

    evens, slots = [], []
    for h in range(2):
        e = (z + NZ - h) % NZ
        evens.append(e % 2)
        slots.append((e // 2 + NX - x) % NX)
    halves = [origin(q) // 4 for q in range(8)]
    parity = [evens[0] + (evens[1] - evens[0]) * h for h in halves]
    slot0 = [slots[0] + (slots[1] - slots[0]) * h for h in halves]
    plus3 = (3 * sigma + 1) // 2
    minus3 = (1 - 3 * sigma) // 2

    def at(q, steps):
        j = (slot0[q] + steps + NX) % NX
        return cb.at[q, core, pl.ds(pl.multiple_of(j * SHARD, SHARD), SHARD), :]

    base = BASE

    def is_even(q):
        return parity[q] == 0

    def pass_on(q, values, slot, sem, dev):
        encode(values, eb.at[q, sem])
        copy_of(eb.at[q, sem], rb.at[q, slot], ssem.at[base + 4 * q + sem], ch.at[q, slot], dev).start()

    def merge(q):
        arrive(xb.at[q], ex.at[q])
        cb[q, core] += xb[q]

    def add_in(q, steps, ref, sem):
        arrive(ref, sem)
        return at(q, steps)[...] + decode(ref)

    def stage1(q):
        @pl.when(is_even(q))
        def _():
            pass_on(q, at(q, 2)[...], 0, 0, ahead)

        @pl.when(jnp.logical_not(is_even(q)))
        def _():
            pass_on(q, at(q, minus3)[...], 1, 1, behind)

    def stage2(q):
        @pl.when(jnp.logical_not(is_even(q)))
        def _():
            pass_on(q, add_in(q, plus3, rb.at[q, 0], ch.at[q, 0]), 0, 0, ahead)

    def stage3(q):
        @pl.when(is_even(q))
        def _():
            for slot, steps, dev in ((1, -sigma, behind), (0, sigma, ahead)):
                pass_on(q, add_in(q, steps, rb.at[q, slot], ch.at[q, slot]), 2 + slot, 1 + slot, dev)

    up, down = (1 + sigma) // 2, (1 - sigma) // 2

    def stage4(q):
        @pl.when(jnp.logical_not(is_even(q)))
        def _():
            for slot, steps, dev in ((1, down, behind), (0, up, ahead)):
                pass_on(q, add_in(q, steps, rb.at[q, 2 + slot], ch.at[q, 2 + slot]), 2 + slot, 2 + slot, dev)

    def straight(q, values, slot, sem, dev):
        f = FAST.index(q)
        encode(values, eb.at[q, sem])
        copy_of(eb.at[q, sem], fb.at[f, slot], ssem.at[base + 4 * q + sem], fch.at[f, slot], dev).start()

    def fast1(q):
        @pl.when(is_even(q))
        def _():
            straight(q, at(q, 2)[...], 0, 0, ahead)
            straight(q, at(q, 1)[...], 3, 1, along_z(2))
            straight(q, at(q, -1)[...], 4, 2, along_z(-2))

        @pl.when(jnp.logical_not(is_even(q)))
        def _():
            straight(q, at(q, minus3)[...], 5 + up, 0, along_z(-3 * sigma))
            straight(q, at(q, 1)[...], 1, 1, along_z(1))
            straight(q, at(q, 0)[...], 2, 2, along_z(-1))

    def fast2(q):
        @pl.when(jnp.logical_not(is_even(q)))
        def _():
            f = FAST.index(q)
            straight(q, add_in(q, plus3, fb.at[f, 0], fch.at[f, 0]), 5 + down, 3, along_z(3 * sigma))

    def place(ref, index):
        columns = pl.ds(pl.multiple_of(core * HALF, HALF), HALF)
        return ref.at[index, :, columns]

    def finish(q):
        origin_y = origin(q)
        index = origin_y % 2
        mine = (origin_y // 2) % 2 == core

        @pl.when(is_even(q))
        def _():
            total = at(q, 0)[...]
            if q in FAST:
                f = FAST.index(q)
                for slot in range(1, 7):
                    arrive(fb.at[f, slot], fch.at[f, slot])
                    total += decode(fb.at[f, slot])
            else:
                for slot in (2, 3):
                    arrive(rb.at[q, slot], ch.at[q, slot])
                    total += decode(rb.at[q, slot])
            total = total.astype(jnp.bfloat16)

            @pl.when(mine)
            def _():
                place(done, index)[...] = total

            @pl.when(jnp.logical_not(mine))
            def _():
                fin[index] = total
                copy_of(fin.at[index], place(done, index), fs.at[0, index], fs.at[1, index], partner).start()

    def mask_rows(part):
        if part == 0:
            load_a.wait()

        def apply_mask(i, carry):
            rows = pl.ds(pl.multiple_of(i * TILE, TILE), TILE)
            for k in range(DEPTH // TILE):
                cols = slice(k * TILE, (k + 1) * TILE)
                a[rows, cols] = jnp.where(mask[i, k] != 0, a[rows, cols], jnp.zeros((TILE, TILE), jnp.bfloat16))
            return carry

        lax.fori_loop(4 * part, 4 * part + 4, apply_mask, 0)

    for step, *args in (
        (own_rest_y,),
        (own_rest_x,),
        (mask_rows, 0),
        (own_first_y,),
        (own_first_x,),
        (relay, 0, 3),
        (relay, 0, 1),
        (take_rest, 2),
        (take_rest, 1),
        (gather, 1),
        (gather, 3),
        (relay, 2, 3),
        (take_first, 1, 0),
        (relay, 2, 1),
        (take_rest, 4),
        (take_rest, 3),
        (take_far, 0),
        (take_first, 2, 1),
        (mask_rows, 1),
        (gather_far,),
        (product, 0, 0),
        (take_first, 1, 1),
        (take_first, 2, 3),
        (product, 0, 1),
        (relay, 1, 1),
        (take_first, 2, 0),
        (take_far, 2),
        (relay, 1, 3),
        (take_first, 1, 3),
        (product, 0, 2),
        (relay, 4, 1),
        (relay, 4, 3),
        (product, 0, 3),
        (take_rest, 5),
        (relay, 3, 3),
        (merge, 0),
        (relay, 3, 1),
        (take_rest, 6),
        (take_first, 1, 2),
        (stage1, 0),
        (take_first, 2, 2),
        (take_first, 4, 1),
        (take_first, 3, 1),
        (take_far, 1),
        (product, 1, 0),
        (product, 1, 1),
        (take_first, 3, 3),
        (take_first, 4, 3),
        (product, 1, 2),
        (take_first, 4, 0),
        (take_first, 3, 0),
        (product, 1, 3),
        (merge, 1),
        (take_rest_far, 5),
        (stage1, 1),
        (merge, 2),
        (stage2, 0),
        (take_far, 4),
        (relay, 5, 1),
        (take_first, 4, 2),
        (relay, 5, 3),
        (stage1, 2),
        (take_far, 3),
        (take_first, 3, 2),
        (product, 3, 0),
        (relay, 6, 3),
        (relay, 6, 1),
        (product, 3, 1),
        (take_rest_far, 6),
        (product, 3, 2),
        (take_first, 5, 3),
        (product, 3, 3),
        (merge, 3),
        (stage2, 1),
        (take_first, 6, 1),
        (merge, 4),
        (stage3, 0),
        (take_first, 5, 0),
        (take_far, 5),
        (take_first, 6, 0),
        (stage1, 4),
        (stage1, 3),
        (take_first, 5, 2),
        (take_first, 6, 2),
        (stage2, 2),
        (take_far, 6),
        (take_first, 5, 1),
        (take_first, 6, 3),
        (product, 5, 0),
        (product, 5, 1),
        (relay, 7, 3),
        (relay, 7, 1),
        (product, 5, 2),
        (product, 5, 3),
        (merge, 5),
        (stage1, 5),
        (merge, 6),
        (stage3, 1),
        (stage1, 6),
        (stage4, 0),
        (take_first, 7, 0),
        (take_first, 7, 1),
        (take_first, 7, 2),
        (stage2, 3),
        (stage2, 4),
        (take_first, 7, 3),
        (stage3, 2),
        (take_far, 7),
        (product, 7, 0),
        (product, 7, 1),
        (product, 7, 2),
        (stage2, 5),
        (product, 7, 3),
        (stage2, 6),
        (merge, 7),
        (fast1, 7),
        (stage3, 4),
        (stage3, 3),
        (stage3, 5),
        (stage3, 6),
        (fast2, 7),
        (stage4, 2),
        (stage4, 1),
        (stage4, 4),
        (stage4, 3),
        (stage4, 5),
        (stage4, 6),
        (finish, 2),
        (finish, 0),
        (finish, 1),
        (finish, 4),
        (finish, 3),
        (finish, 7),
        (finish, 5),
        (finish, 6),
    ):
        step(*args)

    for index in range(2):
        half = pl.ds(pl.multiple_of((1 - core) * HALF, HALF), HALF)
        arrive(done.at[index, :, half], fs.at[1, index])
        copy_of(fin.at[index], place(done, index), fs.at[0, index], fs.at[1, index], partner).wait_send()
    for index in range(2):
        out[index * SHARD : (index + 1) * SHARD, :] = done[index]

    for copy in pending:
        copy.wait_send()
    for q in range(8):
        @pl.when(is_even(q))
        def _():
            for slot in range(3):
                copy_of(rb.at[q, 0], rb.at[q, 0], ssem.at[base + 4 * q + slot], ch.at[q, 0], partner).wait_send()

        @pl.when(jnp.logical_not(is_even(q)))
        def _():
            for slot in range(4):
                copy_of(rb.at[q, 0], rb.at[q, 0], ssem.at[base + 4 * q + slot], ch.at[q, 0], partner).wait_send()


def hand_over(sums, out):
    out[...] = sums[...]


def per_device(amplitudes, integrals, tile_mask):
    result = pl.pallas_call(
        kernel,
        out_shape=jax.ShapeDtypeStruct((2 * SHARD, ROWS), jnp.bfloat16),
        in_specs=[
            pl.BlockSpec(memory_space=pl.ANY),
            pl.BlockSpec(memory_space=pl.ANY),
            pl.BlockSpec(memory_space=pltpu.SMEM),
        ],
        out_specs=pl.BlockSpec(memory_space=pltpu.VMEM),
        scratch_shapes=[
            pltpu.VMEM((ROWS, DEPTH), jnp.bfloat16),
            pltpu.VMEM((8, 4 * SHARD, DEPTH), jnp.bfloat16),
            pltpu.VMEM((8, 2, 4 * SHARD, HALF), jnp.float32),
            pltpu.VMEM((8, 4 * SHARD, HALF), jnp.float32),
            pltpu.VMEM((8, 4, CODED, TILE), jnp.int16),
            pltpu.VMEM((8, 4, CODED, TILE), jnp.int16),
            pltpu.VMEM((len(FAST), 7, CODED, TILE), jnp.int16),
            pltpu.VMEM((2, SHARD, HALF), jnp.bfloat16),
            pltpu.VMEM((2, SHARD, ROWS), jnp.bfloat16),
            pltpu.SemaphoreType.DMA((2,)),
            pltpu.SemaphoreType.DMA((N_SEND,)),
            pltpu.SemaphoreType.DMA((8, 12)),
            pltpu.SemaphoreType.DMA((8,)),
            pltpu.SemaphoreType.DMA((8, 4)),
            pltpu.SemaphoreType.DMA((len(FAST), 7)),
            pltpu.SemaphoreType.DMA((2, 2)),
        ],
        compiler_params=pltpu.CompilerParams(
            collective_id=0, has_side_effects=True, vmem_limit_bytes=60 * 1024 * 1024
        ),
    )(amplitudes, integrals.T, tile_mask)
    return pl.pallas_call(
        hand_over,
        out_shape=jax.ShapeDtypeStruct(result.shape, result.dtype),
        in_specs=[pl.BlockSpec(memory_space=pltpu.VMEM)],
        out_specs=pl.BlockSpec(memory_space=pltpu.VMEM),
    )(result).T


def solution(mesh):
    placed = (P("row", "col"), P("col", "row"), P("row", "col"))
    return jax.shard_map(
        per_device, mesh=mesh, in_specs=placed, out_specs=P("row", "col"), check_vma=False
    )
```

```python
import jax
import jax.numpy as jnp
from jax import lax
from jax.experimental import pallas as pl
from jax.experimental.pallas import tpu as pltpu
from jax.sharding import PartitionSpec as P

MESH = pl.DeviceIdType.MESH
NX, NY, NZ = 4, 8, 8
TILE = 128
SHARD = 32
ROWS = 1024
DEPTH = 2048
HALF = ROWS // 2
LEVELS = 32000.0
CODED = SHARD * HALF // TILE + 16
BLOCK = 256
SPLIT = 768

FIRST = slice(0, SPLIT)
REST = slice(SPLIT, DEPTH)
FIRST_A = slice(0, SPLIT // 2)
FIRST_B = slice(SPLIT // 2, SPLIT)
REST_A = slice(SPLIT, (SPLIT + DEPTH) // 2)
REST_B = slice((SPLIT + DEPTH) // 2, DEPTH)
BASE = 100
N_SEND = BASE + 32
FAST = (6, 7)


def shard(j):
    return slice(j * SHARD, (j + 1) * SHARD)


def kernel(a_hbm, own, mask, out, a, bt, cb, xb, eb, rb, fb, fin, done, lsem, ssem, ag, ex, ch, fch, fs):
    row, col = lax.axis_index("row"), lax.axis_index("col")
    x, y = row // NY, row % NY
    z, core = col // 2, col % 2
    xp = (((x + 1) % NX) * NY + y, col)
    xm = (((x + NX - 1) % NX) * NY + y, col)
    yp = (x * NY + (y + 1) % NY, col)
    ym = (x * NY + (y + NY - 1) % NY, col)
    sigma = 1 - 2 * core
    ahead = (row, ((z + NZ + sigma) % NZ) * 2 + core)
    behind = (row, ((z + NZ - sigma) % NZ) * 2 + core)
    partner = (row, z * 2 + 1 - core)

    def along_z(delta):
        return (row, ((z + NZ + delta) % NZ) * 2 + core)


    load_a = pltpu.make_async_copy(a_hbm, a, lsem.at[0])
    load_b = pltpu.make_async_copy(own, bt.at[0, shard(0)], lsem.at[1])
    load_a.start()
    load_b.start()

    barrier = pltpu.get_barrier_semaphore()
    for dev in [xp, xm, yp, ym, partner] + [along_z(d) for d in (1, -1, 2, -2, 3, -3)]:
        pl.semaphore_signal(barrier, inc=1, device_id=dev, device_id_type=MESH)
    pl.semaphore_wait(barrier, 11)

    pending = []
    count = [0]

    def copy_of(src, dst, send_sem, recv_sem, dev):
        return pltpu.make_async_remote_copy(
            src_ref=src, dst_ref=dst, send_sem=send_sem, recv_sem=recv_sem, device_id=dev, device_id_type=MESH
        )

    def send(src, dst, recv_sem, dev):
        copy = copy_of(src, dst, ssem.at[count[0]], recv_sem, dev)
        count[0] += 1
        copy.start()
        pending.append(copy)

    def arrive(dst, recv_sem):
        copy_of(dst, dst, ssem.at[0], recv_sem, partner).wait_recv()

    def origin(q):
        step = (q + 1) // 2
        return (y + NY - step) % NY if q % 2 == 1 else (y + step) % NY

    def own_first_x():
        for dev, j, k in ((xp, 3, 2), (xm, 1, 3)):
            send(own.at[:, FIRST], bt.at[0, shard(j), FIRST], ag.at[0, k], dev)

    def own_rest_y():
        for dev, q in ((yp, 1), (ym, 2)):
            send(own.at[:, REST], bt.at[q, shard(0), REST], ag.at[q, 0], dev)

    def own_first_y():
        for dev, q in ((yp, 1), (ym, 2)):
            send(own.at[:, FIRST], bt.at[q, shard(0), FIRST], ag.at[q, 2], dev)

    def across_a(q, src):
        send(src.at[:, REST_A], bt.at[q, shard(3), REST_A], ag.at[q, 6], xp)
        send(src.at[:, REST_A], bt.at[q, shard(1), REST_A], ag.at[q, 10], xm)

    def across_b(q, src):
        send(src.at[:, REST_B], bt.at[q, shard(1), REST_B], ag.at[q, 7], xm)
        send(src.at[:, REST_B], bt.at[q, shard(3), REST_B], ag.at[q, 11], xp)

    def across(q, src):
        send(src.at[:, REST_A], bt.at[q, shard(3), REST_A], ag.at[q, 6], xp)
        send(src.at[:, REST_B], bt.at[q, shard(1), REST_B], ag.at[q, 7], xm)
        send(src.at[:, REST_B], bt.at[q, shard(3), REST_B], ag.at[q, 11], xp)
        send(src.at[:, REST_A], bt.at[q, shard(1), REST_A], ag.at[q, 10], xm)

    def own_rest_x():
        across(0, own)

    def gather(j):
        dev, half, k = (xp, FIRST_A, 4) if j == 3 else (xm, FIRST_B, 5)
        arrive(bt.at[0, shard(j), FIRST], ag.at[0, 2 if j == 3 else 3])
        send(bt.at[0, shard(j), half], bt.at[0, shard(2), half], ag.at[0, k], dev)
        for dev, q in ((yp, 1), (ym, 2)):
            send(bt.at[0, shard(j), FIRST], bt.at[q, shard(j), FIRST], ag.at[q, 2 + j], dev)

    def gather_far():
        arrive(bt.at[0, shard(2), FIRST_A], ag.at[0, 4])
        arrive(bt.at[0, shard(2), FIRST_B], ag.at[0, 5])
        for dev, q in ((yp, 1), (ym, 2)):
            send(bt.at[0, shard(2), FIRST], bt.at[q, shard(2), FIRST], ag.at[q, 4], dev)

    def take_rest(q):
        dev = yp if q % 2 == 1 else ym
        arrive(bt.at[q, shard(0), REST], ag.at[q, 0])
        if q < 5:
            send(bt.at[q, shard(0), REST], bt.at[q + 2, shard(0), REST], ag.at[q + 2, 0], dev)
        elif q == 5:
            send(bt.at[5, shard(0), REST_A], bt.at[7, shard(0), REST_A], ag.at[7, 0], dev)
        else:
            send(bt.at[6, shard(0), REST_B], bt.at[7, shard(0), REST_B], ag.at[7, 1], dev)
        across(q, bt.at[q, shard(0)])

    def take_rest_far(source):
        if source == 5:
            arrive(bt.at[7, shard(0), REST_A], ag.at[7, 0])
            across_a(7, bt.at[7, shard(0)])
        else:
            arrive(bt.at[7, shard(0), REST_B], ag.at[7, 1])
            across_b(7, bt.at[7, shard(0)])

    def take_first(q, j):
        dev = yp if q % 2 == 1 else ym
        arrive(bt.at[q, shard(j), FIRST], ag.at[q, 2 + j])
        if q < 5:
            send(bt.at[q, shard(j), FIRST], bt.at[q + 2, shard(j), FIRST], ag.at[q + 2, 2 + j], dev)
        elif (q == 5 and j in (0, 3)) or (q == 6 and j in (1, 2)):
            send(bt.at[q, shard(j), FIRST], bt.at[7, shard(j), FIRST], ag.at[7, 2 + j], dev)

    def relay(q, j):
        if j == 3:
            arrive(bt.at[q, shard(3), REST_A], ag.at[q, 6])
            send(bt.at[q, shard(3), REST_A], bt.at[q, shard(2), REST_A], ag.at[q, 8], xp)
        else:
            arrive(bt.at[q, shard(1), REST_B], ag.at[q, 7])
            send(bt.at[q, shard(1), REST_B], bt.at[q, shard(2), REST_B], ag.at[q, 9], xm)

    def take_far(q):
        arrive(bt.at[q, shard(1), REST_A], ag.at[q, 10])
        arrive(bt.at[q, shard(3), REST_B], ag.at[q, 11])
        arrive(bt.at[q, shard(2), REST_A], ag.at[q, 8])
        arrive(bt.at[q, shard(2), REST_B], ag.at[q, 9])

    def product(q, i):
        if q == 0 and i == 0:
            load_b.wait()
        multiply(q, 1 - core if i < 2 else core, i % 2)
        if i == 1:
            for row_slot in (q,) if q in (0, 7) else (q, q + 1):
                swap(row_slot)

    def multiply(q, which, i):
        start = pl.multiple_of(which * HALF + i * BLOCK, BLOCK)
        n = 1 if q in (0, 7) else 2
        sums = lax.dot_general(
            bt[q : q + n].reshape(n * 4 * SHARD, DEPTH),
            a[pl.ds(start, BLOCK), :],
            (((1,), (1,)), ((), ())),
            preferred_element_type=jnp.float32,
        )
        for r in range(n):
            cb[q + r, which, :, i * BLOCK : (i + 1) * BLOCK] = sums[r * 4 * SHARD : (r + 1) * 4 * SHARD]

    def swap(q):
        send(cb.at[q, 1 - core], xb.at[q], ex.at[q], partner)

    def encode(values, ref):
        parts = [values[:, m * TILE : (m + 1) * TILE].reshape(SHARD // 8, 8, TILE) for m in range(HALF // TILE)]
        top = jnp.max(jnp.abs(parts[0]), axis=0)
        for part in parts[1:]:
            top = jnp.maximum(top, jnp.max(jnp.abs(part), axis=0))
        power = jnp.ceil(jnp.log2(jnp.maximum(top, 1e-30)))
        scale = (jnp.exp2(-power) * LEVELS)[None]
        for m, part in enumerate(parts):
            whole = jnp.round(part * scale).reshape(SHARD, TILE)
            ref[m * SHARD : (m + 1) * SHARD, :] = whole.astype(jnp.int32).astype(jnp.int16)
        both = jnp.concatenate([power, power], axis=0)
        ref[CODED - 16 :, :] = both.astype(jnp.int32).astype(jnp.int16)

    def decode(ref):
        power = ref[CODED - 16 :, :].astype(jnp.int32).astype(jnp.float32)[:8]
        step = (jnp.exp2(power) * (1.0 / LEVELS))[None]
        parts = []
        for m in range(HALF // TILE):
            whole = ref[m * SHARD : (m + 1) * SHARD, :].astype(jnp.int32).astype(jnp.float32)
            parts.append((whole.reshape(SHARD // 8, 8, TILE) * step).reshape(SHARD, TILE))
        return jnp.concatenate(parts, axis=1)

    evens, slots = [], []
    for h in range(2):
        e = (z + NZ - h) % NZ
        evens.append(e % 2)
        slots.append((e // 2 + NX - x) % NX)
    halves = [origin(q) // 4 for q in range(8)]
    parity = [evens[0] + (evens[1] - evens[0]) * h for h in halves]
    slot0 = [slots[0] + (slots[1] - slots[0]) * h for h in halves]
    plus3 = (3 * sigma + 1) // 2
    minus3 = (1 - 3 * sigma) // 2

    def at(q, steps):
        j = (slot0[q] + steps + NX) % NX
        return cb.at[q, core, pl.ds(pl.multiple_of(j * SHARD, SHARD), SHARD), :]

    base = BASE

    def is_even(q):
        return parity[q] == 0

    def pass_on(q, values, slot, sem, dev):
        encode(values, eb.at[q, sem])
        copy_of(eb.at[q, sem], rb.at[q, slot], ssem.at[base + 4 * q + sem], ch.at[q, slot], dev).start()

    def merge(q):
        arrive(xb.at[q], ex.at[q])
        cb[q, core] += xb[q]

    def add_in(q, steps, ref, sem):
        arrive(ref, sem)
        return at(q, steps)[...] + decode(ref)

    def stage1(q):
        @pl.when(is_even(q))
        def _():
            pass_on(q, at(q, 2)[...], 0, 0, ahead)

        @pl.when(jnp.logical_not(is_even(q)))
        def _():
            pass_on(q, at(q, minus3)[...], 1, 1, behind)

    def stage2(q):
        @pl.when(jnp.logical_not(is_even(q)))
        def _():
            pass_on(q, add_in(q, plus3, rb.at[q, 0], ch.at[q, 0]), 0, 0, ahead)

    def stage3(q):
        @pl.when(is_even(q))
        def _():
            for slot, steps, dev in ((1, -sigma, behind), (0, sigma, ahead)):
                pass_on(q, add_in(q, steps, rb.at[q, slot], ch.at[q, slot]), 2 + slot, 1 + slot, dev)

    up, down = (1 + sigma) // 2, (1 - sigma) // 2

    def stage4(q):
        @pl.when(jnp.logical_not(is_even(q)))
        def _():
            for slot, steps, dev in ((1, down, behind), (0, up, ahead)):
                pass_on(q, add_in(q, steps, rb.at[q, 2 + slot], ch.at[q, 2 + slot]), 2 + slot, 2 + slot, dev)

    def straight(q, values, slot, sem, dev):
        f = FAST.index(q)
        encode(values, eb.at[q, sem])
        copy_of(eb.at[q, sem], fb.at[f, slot], ssem.at[base + 4 * q + sem], fch.at[f, slot], dev).start()

    def fast1(q):
        @pl.when(is_even(q))
        def _():
            straight(q, at(q, 2)[...], 0, 0, ahead)
            straight(q, at(q, 1)[...], 3, 1, along_z(2))
            straight(q, at(q, -1)[...], 4, 2, along_z(-2))

        @pl.when(jnp.logical_not(is_even(q)))
        def _():
            straight(q, at(q, minus3)[...], 5 + up, 0, along_z(-3 * sigma))
            straight(q, at(q, 1)[...], 1, 1, along_z(1))
            straight(q, at(q, 0)[...], 2, 2, along_z(-1))

    def fast2(q):
        @pl.when(jnp.logical_not(is_even(q)))
        def _():
            f = FAST.index(q)
            straight(q, add_in(q, plus3, fb.at[f, 0], fch.at[f, 0]), 5 + down, 3, along_z(3 * sigma))

    def place(ref, index):
        columns = pl.ds(pl.multiple_of(core * HALF, HALF), HALF)
        return ref.at[index, :, columns]

    def finish(q):
        origin_y = origin(q)
        index = origin_y % 2
        mine = (origin_y // 2) % 2 == core

        @pl.when(is_even(q))
        def _():
            total = at(q, 0)[...]
            if q in FAST:
                f = FAST.index(q)
                for slot in range(1, 7):
                    arrive(fb.at[f, slot], fch.at[f, slot])
                    total += decode(fb.at[f, slot])
            else:
                for slot in (2, 3):
                    arrive(rb.at[q, slot], ch.at[q, slot])
                    total += decode(rb.at[q, slot])
            total = total.astype(jnp.bfloat16)

            @pl.when(mine)
            def _():
                place(done, index)[...] = total

            @pl.when(jnp.logical_not(mine))
            def _():
                fin[index] = total
                copy_of(fin.at[index], place(done, index), fs.at[0, index], fs.at[1, index], partner).start()

    def mask_rows(part):
        if part == 0:
            load_a.wait()

        def apply_mask(i, carry):
            rows = pl.ds(pl.multiple_of(i * TILE, TILE), TILE)
            for k in range(DEPTH // TILE):
                cols = slice(k * TILE, (k + 1) * TILE)
                a[rows, cols] = jnp.where(mask[i, k] != 0, a[rows, cols], jnp.zeros((TILE, TILE), jnp.bfloat16))
            return carry

        lax.fori_loop(4 * part, 4 * part + 4, apply_mask, 0)

    for step, *args in (
        (own_first_x,),
        (own_rest_y,),
        (own_first_y,),
        (own_rest_x,),
        (gather, 3),
        (gather, 1),
        (relay, 0, 3),
        (relay, 0, 1),
        (take_rest, 2),
        (mask_rows, 0),
        (take_rest, 1),
        (gather_far,),
        (take_first, 2, 3),
        (take_first, 1, 3),
        (mask_rows, 1),
        (relay, 2, 3),
        (relay, 2, 1),
        (take_rest, 4),
        (take_rest, 3),
        (take_first, 1, 0),
        (take_first, 2, 1),
        (relay, 1, 3),
        (relay, 1, 1),
        (take_first, 2, 2),
        (take_first, 3, 3),
        (take_far, 0),
        (take_first, 1, 2),
        (take_first, 4, 3),
        (product, 0, 0),
        (product, 0, 1),
        (product, 0, 2),
        (relay, 4, 3),
        (relay, 4, 1),
        (take_rest, 6),
        (take_far, 2),
        (take_first, 1, 1),
        (product, 0, 3),
        (merge, 0),
        (take_first, 2, 0),
        (relay, 3, 3),
        (relay, 3, 1),
        (take_rest, 5),
        (stage1, 0),
        (take_first, 3, 0),
        (take_far, 1),
        (take_first, 4, 1),
        (product, 1, 0),
        (take_first, 4, 2),
        (take_first, 6, 3),
        (product, 1, 1),
        (take_first, 3, 2),
        (product, 1, 2),
        (take_rest_far, 6),
        (take_first, 5, 3),
        (relay, 6, 1),
        (product, 1, 3),
        (relay, 6, 3),
        (take_first, 3, 1),
        (merge, 1),
        (stage1, 1),
        (merge, 2),
        (take_first, 4, 0),
        (stage1, 2),
        (take_rest_far, 5),
        (stage2, 0),
        (take_far, 4),
        (relay, 5, 3),
        (take_far, 3),
        (relay, 5, 1),
        (product, 3, 0),
        (product, 3, 1),
        (take_first, 6, 1),
        (product, 3, 2),
        (product, 3, 3),
        (merge, 3),
        (stage2, 1),
        (merge, 4),
        (take_first, 7, 3),
        (take_first, 5, 0),
        (stage1, 3),
        (stage1, 4),
        (take_first, 6, 0),
        (take_first, 5, 2),
        (take_first, 5, 1),
        (take_far, 6),
        (stage2, 2),
        (relay, 7, 3),
        (relay, 7, 1),
        (stage3, 0),
        (take_first, 6, 2),
        (take_far, 5),
        (product, 5, 0),
        (product, 5, 1),
        (product, 5, 2),
        (product, 5, 3),
        (merge, 5),
        (stage1, 5),
        (merge, 6),
        (stage3, 1),
        (take_first, 7, 1),
        (fast1, 6),
        (take_first, 7, 2),
        (take_far, 7),
        (take_first, 7, 0),
        (product, 7, 0),
        (product, 7, 1),
        (stage2, 4),
        (stage2, 3),
        (product, 7, 2),
        (product, 7, 3),
        (stage2, 5),
        (merge, 7),
        (fast1, 7),
        (fast2, 6),
        (stage3, 2),
        (stage3, 4),
        (stage3, 3),
        (stage3, 5),
        (fast2, 7),
        (stage4, 1),
        (stage4, 0),
        (stage4, 2),
        (stage4, 4),
        (stage4, 3),
        (stage4, 5),
        (finish, 6),
        (finish, 0),
        (finish, 1),
        (finish, 2),
        (finish, 7),
        (finish, 3),
        (finish, 4),
        (finish, 5),
    ):
        step(*args)

    for index in range(2):
        half = pl.ds(pl.multiple_of((1 - core) * HALF, HALF), HALF)
        arrive(done.at[index, :, half], fs.at[1, index])
        copy_of(fin.at[index], place(done, index), fs.at[0, index], fs.at[1, index], partner).wait_send()
    for index in range(2):
        out[index * SHARD : (index + 1) * SHARD, :] = done[index]

    for copy in pending:
        copy.wait_send()
    for q in range(8):
        @pl.when(is_even(q))
        def _():
            for slot in range(3):
                copy_of(rb.at[q, 0], rb.at[q, 0], ssem.at[base + 4 * q + slot], ch.at[q, 0], partner).wait_send()

        @pl.when(jnp.logical_not(is_even(q)))
        def _():
            for slot in range(4):
                copy_of(rb.at[q, 0], rb.at[q, 0], ssem.at[base + 4 * q + slot], ch.at[q, 0], partner).wait_send()


def hand_over(sums, out):
    out[...] = sums[...]


def per_device(amplitudes, integrals, tile_mask):
    result = pl.pallas_call(
        kernel,
        out_shape=jax.ShapeDtypeStruct((2 * SHARD, ROWS), jnp.bfloat16),
        in_specs=[
            pl.BlockSpec(memory_space=pl.ANY),
            pl.BlockSpec(memory_space=pl.ANY),
            pl.BlockSpec(memory_space=pltpu.SMEM),
        ],
        out_specs=pl.BlockSpec(memory_space=pltpu.VMEM),
        scratch_shapes=[
            pltpu.VMEM((ROWS, DEPTH), jnp.bfloat16),
            pltpu.VMEM((8, 4 * SHARD, DEPTH), jnp.bfloat16),
            pltpu.VMEM((8, 2, 4 * SHARD, HALF), jnp.float32),
            pltpu.VMEM((8, 4 * SHARD, HALF), jnp.float32),
            pltpu.VMEM((8, 4, CODED, TILE), jnp.int16),
            pltpu.VMEM((8, 4, CODED, TILE), jnp.int16),
            pltpu.VMEM((len(FAST), 7, CODED, TILE), jnp.int16),
            pltpu.VMEM((2, SHARD, HALF), jnp.bfloat16),
            pltpu.VMEM((2, SHARD, ROWS), jnp.bfloat16),
            pltpu.SemaphoreType.DMA((2,)),
            pltpu.SemaphoreType.DMA((N_SEND,)),
            pltpu.SemaphoreType.DMA((8, 12)),
            pltpu.SemaphoreType.DMA((8,)),
            pltpu.SemaphoreType.DMA((8, 4)),
            pltpu.SemaphoreType.DMA((len(FAST), 7)),
            pltpu.SemaphoreType.DMA((2, 2)),
        ],
        compiler_params=pltpu.CompilerParams(
            collective_id=0, has_side_effects=True, vmem_limit_bytes=60 * 1024 * 1024
        ),
    )(amplitudes, integrals.T, tile_mask)
    return pl.pallas_call(
        hand_over,
        out_shape=jax.ShapeDtypeStruct(result.shape, result.dtype),
        in_specs=[pl.BlockSpec(memory_space=pltpu.VMEM)],
        out_specs=pl.BlockSpec(memory_space=pltpu.VMEM),
    )(result).T


def solution(mesh):
    placed = (P("row", "col"), P("col", "row"), P("row", "col"))
    return jax.shard_map(
        per_device, mesh=mesh, in_specs=placed, out_specs=P("row", "col"), check_vma=False
    )
```
